32 devices in a mesh: owner: 16 (over z, x, core), dense: 2 (over y).
Axes of the slice: x: 2, y: 2, z: 4, core: 2. Of those that a mesh axis runs over, the one named last changes fastest.
Arguments:
- owners: int32 [8192, 13, 4], P(('owner', 'dense')), may hold values from 0 to 15, all different within a row; in each aligned block of 3328 rows (0 to 3327, 3328 to 6655, ..., all dimensions but the last counted through in order) at most 1664 rows name the same one
- local_rows: int32 [8192, 13, 4], P(('owner', 'dense')), may hold values from 0 to 2047, as said below
- weights: float32 [8192, 13, 4], P(('owner', 'dense')), may hold values from 0.25 to 4
- labels: bfloat16 [8192], P(('owner', 'dense')), may hold values from 0 to 1
- table: float32 [32768, 128], P('owner'), may hold values from -6 to 6
- accum: float32 [32768], P('owner'), may hold values from 0.0001 to 0.01
- w_in: bfloat16 [1664, 4096], P(None, 'dense'), may hold values from -0.15625 to 0.15625
- b_in: bfloat16 [4096], P('dense'), may hold values from -3 to 3
- w_out: bfloat16 [4096], P('dense'), may hold values from -0.29882812 to 0.29882812
Outputs:
- new_table: float32 [32768, 128], P('owner')
- new_accum: float32 [32768], P('owner')
- weight_grad: float32 [8192, 13, 4], P(('owner', 'dense'))
The draws below stay inside these ranges and needn't reach their ends.
Inputs may be any that keep to these rules, and one draw needn't show every extreme that they name: The 4 owners of one bag differ. Among the bags of one device (3328 of them, aligned blocks of rows), at most 1664 name one owner. Among the ids of one device's samples (13312 of them, aligned blocks of rows), exactly 416 distinct values of local_rows occur.
All inputs are finite; a program needn't handle non-finite values.
Results may differ from the reference program's by a relative error of at most 0.0056.
Values may be sent and summed in bfloat16 or wider, within the bound.
A program may use at most 128 MiB of HBM per device.

```python
import math
import jax
import jax.numpy as jnp
import numpy as np
from jax import lax

E = 128
F = 13
L = 4
H = 4096
S_DEV = 256
ROWS_DEV = 2048
CAP = 1664
UNIQ = 416
SAMPLES = 8192
ROWS = 32768
N_OWNER = 16


def draw_local_rows(key, part):
    device_count = SAMPLES // S_DEV
    per_device = S_DEV * F * L

    def one_device(dev_key):
        pool_key, first_key, second_key = jax.random.split(dev_key, 3)
        pool = jax.random.permutation(pool_key, ROWS_DEV)[:UNIQ]
        first_pick = jax.random.randint(first_key, (per_device,), 0, UNIQ)
        second_pick = jax.random.randint(second_key, (per_device,), 0, UNIQ)
        picked = jnp.minimum(first_pick, second_pick)
        picked = picked.at[:UNIQ].set(jnp.arange(UNIQ, dtype=picked.dtype))
        return pool[picked]
    dev_keys = jax.random.split(jax.random.fold_in(key, 71), device_count)
    return jax.vmap(one_device)(dev_keys).reshape(SAMPLES, F, L).astype(jnp.int32)


def shard_levels(own_key, shape, cuts, smallest, high):
    factor_of = 1.0
    for axis_at, shards_of in cuts:
        heights = jax.random.uniform(jax.random.fold_in(jax.random.fold_in(own_key, 6), axis_at), (shards_of,), jnp.float32, smallest / len(cuts), high / len(cuts))
        factor_of = factor_of * jnp.repeat(jnp.exp(heights), shape[axis_at] // shards_of).reshape((-1,) + (1,) * (len(shape) - 1 - axis_at))
    return factor_of


def deal_out(own_key, own, number, rows, amount, top, bound, lean):
    order = jax.random.permutation(own_key, amount)
    heavy_load, usual = load_shares(amount, rows * top, bound, lean, True), load_shares(amount, rows * top, bound, lean, False)
    places = jnp.arange(amount)

    def named(tallies, offset_by):
        used = int((tallies > 0).sum())
        fixed = max(1, used // 4)
        shifted = fixed + (places - fixed + offset_by * (used - fixed)) % max(1, amount - fixed)
        return jnp.zeros((amount,), jnp.int32).at[order[jnp.where(places < fixed, places, shifted)]].set(jnp.asarray(tallies, jnp.int32))

    tallies = jnp.where(number % 4 == 0, named(heavy_load, number // 4), named(usual, number - number // 4 - 1))
    mixed = jax.random.permutation(jax.random.fold_in(own, 3), amount)
    source_of, taker = mixed[0:amount // 2 * 2:2], mixed[1:amount // 2 * 2:2]
    slack = jnp.minimum(tallies[source_of] - 1, bound - tallies[taker]) // 2
    slack = jnp.where((source_of == order[0]) | (taker == order[0]) | (tallies[taker] == 0), 0, jnp.maximum(slack, 0))
    shifted = jax.random.randint(jax.random.fold_in(own, 4), (amount // 2,), 0, 1 << 20) % (slack + 1)
    tallies = tallies.at[source_of].add(-shifted).at[taker].add(shifted)
    items = jnp.searchsorted(jnp.cumsum(tallies), jnp.arange(rows * top), side="right").astype(jnp.int32)
    grid = items.reshape(top, rows).T
    grid = grid[jax.random.permutation(jax.random.fold_in(own, 1), rows)]
    offset_by = jax.random.randint(jax.random.fold_in(own, 2), (rows, 1), 0, top)
    return jnp.take_along_axis(grid, (jnp.arange(top)[None, :] + offset_by) % top, axis=1)


def load_shares(amount, total, reach, lean, full):
    portions = [(1 << 20) // math.isqrt(rank ** lean) + 1 for rank in range(1, amount + 1)]
    largest = reach if full else min(reach, max(-(-total // amount), total * portions[0] // sum(portions)))
    least = 1 if total - largest >= amount - 1 else 0
    holding, spare = [largest] + [least] * (amount - 1), total - largest - least * (amount - 1)
    while spare > 0:
        free = [i for i in range(1, amount) if holding[i] < largest] or [i for i in range(1, amount) if holding[i] < reach]
        whole, budget = sum([portions[i] for i in free]), spare
        for i in free:
            addition = min(reach - holding[i], max(1, budget * portions[i] // whole), spare)
            holding[i] = holding[i] + addition
            spare = spare - addition
    return np.array(holding)


def centred(stream_key, shape, width, bound, cuts=(), kind=jnp.bfloat16):
    gain = shard_levels(stream_key, shape, cuts, -0.22, 0.18) if cuts else 1.0
    values = jax.random.normal(stream_key, shape, jnp.float32) * width * gain
    return jnp.minimum(jnp.maximum(values, -bound), bound).astype(kind)


def setup_inputs(seed: int = 0) -> dict:
    seeds = jax.random.split(jax.random.key(seed), 10)
    owners_keys = jax.random.split(jax.random.fold_in(seeds[0], 1), SAMPLES * F // (S_DEV * F))
    owners_turns = jax.random.permutation(jax.random.fold_in(seeds[0], 3), SAMPLES * F // (S_DEV * F))
    owners = jax.vmap(lambda own, number: deal_out(jax.random.fold_in(seeds[0], 2), own, number, S_DEV * F, N_OWNER, L, CAP, 2))(owners_keys, owners_turns).reshape((SAMPLES, F, L))
    local_rows = draw_local_rows(jax.random.fold_in(seeds[9], 71), 0)
    weights = jnp.clip(jnp.exp(math.log(4.0) - 2.7725887 * jax.random.uniform(seeds[2], (SAMPLES, F, L), jnp.float32) ** shard_levels(seeds[2], (SAMPLES, F, L), ((0, 32),), -0.2, 0.2)), 0.25, 4.0)
    labels = jnp.clip(1.0 * jax.random.uniform(seeds[3], (SAMPLES,), jnp.float32) ** shard_levels(seeds[3], (SAMPLES,), ((0, 32),), -0.2, 0.2), 0.0, 1.0).astype(jnp.bfloat16)
    table = centred(seeds[4], (ROWS, E), 1.0, 6.0, ((0, 16),), jnp.float32)
    accum = jnp.clip(jnp.exp(math.log(0.01) - 4.6051702 * jax.random.uniform(seeds[5], (ROWS,), jnp.float32) ** shard_levels(seeds[5], (ROWS,), ((0, 16),), -0.2, 0.2)), 0.0001, 0.01)
    w_in = centred(seeds[6], (F * E, H), (F * E) ** -0.5, 0.15625, ((1, 2),))
    b_in = centred(seeds[7], (H,), 0.5, 3.0, ((0, 2),))
    w_out = centred(seeds[8], (H,), 0.05, 0.29882812, ((0, 2),))
    return dict(owners=owners, local_rows=local_rows, weights=weights, labels=labels, table=table, accum=accum, w_in=w_in, b_in=b_in, w_out=w_out)


step_size = 0.5

def reference(owners, local_rows, weights, labels, table, accum, w_in, b_in, w_out):
    block_rows = math.gcd(SAMPLES, 1024)
    block_count = SAMPLES // block_rows
    row_ids = (owners * ROWS_DEV + local_rows).astype(jnp.int32)
    bias = b_in.astype(jnp.float32)
    out_proj = w_out.astype(jnp.float32)

    def accumulate(row_grad, blocks):
        block_ids, bag_weights, bag_labels = blocks
        looked = table[block_ids].astype(jnp.bfloat16)
        looked_f = looked.astype(jnp.float32)
        weight_sums = lax.optimization_barrier(jnp.sum(bag_weights, axis=-1))
        pooled = lax.optimization_barrier(jnp.sum(bag_weights[..., None] * looked_f, axis=2)) / weight_sums[..., None]
        inputs = pooled.astype(jnp.bfloat16).reshape(block_rows, F * E)
        preact = jnp.dot(inputs, w_in, preferred_element_type=jnp.float32) + bias
        sigma_pre = jax.nn.sigmoid(preact)
        logits = lax.optimization_barrier(jnp.sum(preact * sigma_pre * out_proj, axis=-1))
        logit_grad = jax.nn.sigmoid(logits) - bag_labels.astype(jnp.float32)
        slope = sigma_pre * (1.0 + preact * (1.0 - sigma_pre))
        dhidden = (logit_grad[:, None] * out_proj * slope).astype(jnp.bfloat16)
        dinputs = lax.dot_general(dhidden, w_in, (((1,), (1,)), ((), ())), preferred_element_type=jnp.float32)
        dpooled = dinputs.reshape(block_rows, F, E)
        along = lax.optimization_barrier(jnp.sum(looked_f * dpooled[:, :, None, :], axis=-1))
        centre = lax.optimization_barrier(jnp.sum(pooled * dpooled, axis=-1))
        weight_grads = (along - centre[..., None]) / weight_sums[..., None]
        slot_grad = ((bag_weights / weight_sums[..., None])[..., None] * dpooled[:, :, None, :]).astype(jnp.bfloat16)
        row_grad = row_grad.at[block_ids.reshape(-1)].add(slot_grad.reshape(-1, E).astype(jnp.float32))
        return (row_grad, weight_grads)
    start_grad = jnp.zeros((ROWS_DEV * N_OWNER, E), jnp.float32)
    row_grad, weight_grads = lax.scan(accumulate, start_grad, (row_ids.reshape(block_count, block_rows, F, L), weights.reshape(block_count, block_rows, F, L), labels.reshape(block_count, block_rows)))
    new_accum = accum + lax.optimization_barrier(jnp.mean(row_grad * row_grad, axis=-1))
    new_table = table - step_size * row_grad / jnp.sqrt(new_accum)[:, None]
    return (new_table, new_accum, weight_grads.reshape(SAMPLES, F, L))
```

```python
import functools

import jax
import jax.numpy as jnp
from jax import lax
from jax.experimental import pallas as pl
from jax.experimental.pallas import tpu as pltpu
from jax.sharding import PartitionSpec as P

step_size = 0.5
lane = 128
folds = 4
f32 = jnp.float32
bf16 = jnp.bfloat16
i32 = jnp.int32
MESH = pl.DeviceIdType.MESH
room = 48 * 1024 * 1024


def vmem():
    return pl.BlockSpec(memory_space=pltpu.VMEM)


def partner(me, k, groups):
    peer = me
    bit = 1
    while bit < groups:
        flip = lax.rem(lax.div(k, bit), 2)
        peer = peer + bit * flip * (1 - 2 * lax.rem(lax.div(me, bit), 2))
        bit *= 2
    return peer


def far_first(i, groups):
    half = groups // 2
    return lax.rem(i + half, groups) + lax.div(i, half)


def distinct_body(table_rows, uniq, own_ref, loc_ref, w_ref, row_ref, pos_ref, wo_ref, lows):
    bag_len, bags = own_ref.shape
    groups = pos_ref.shape[0]
    padded = row_ref.shape[1]
    highs = table_rows // lane
    counts = jnp.zeros((highs, lane), f32)
    low_at = lax.broadcasted_iota(i32, (lane, bags), 0)
    high_at = lax.broadcasted_iota(i32, (highs, bags), 0)
    for slot in range(bag_len):
        loc = loc_ref[slot : slot + 1, :]
        low = jnp.where(jnp.bitwise_and(loc, lane - 1) == low_at, 1.0, 0.0).astype(bf16)
        lows[slot] = low
        high = jnp.where(jnp.right_shift(loc, 7) == high_at, 1.0, 0.0).astype(bf16)
        counts += lax.dot_general(high, low, (((1,), (1,)), ((), ())), preferred_element_type=f32)
    present = jnp.where(counts > 0.0, 1.0, 0.0)
    upper = jnp.where(
        lax.broadcasted_iota(i32, (lane, lane), 0) <= lax.broadcasted_iota(i32, (lane, lane), 1),
        1.0,
        0.0,
    ).astype(bf16)
    below = jnp.where(
        lax.broadcasted_iota(i32, (highs, highs), 0) > lax.broadcasted_iota(i32, (highs, highs), 1),
        1.0,
        0.0,
    ).astype(bf16)
    inclusive = jnp.dot(present.astype(bf16), upper, preferred_element_type=f32)
    before = jnp.sum(
        jnp.dot(below, present.astype(bf16), preferred_element_type=f32), axis=1, keepdims=True
    )
    ranks = jnp.where(present > 0.0, inclusive + before - 1.0, -1.0)
    place = lax.broadcasted_iota(i32, (padded, lane), 0).astype(f32)
    lane_at = lax.broadcasted_iota(i32, (1, lane), 1).astype(f32)
    found = jnp.where(place < float(uniq), 0.0, -1.0)
    for h in range(highs):
        found += jnp.where(place == ranks[h : h + 1, :], lane_at + float(h * lane), 0.0)
    column = jnp.sum(found, axis=1, keepdims=True)
    column = jnp.where(place[:, :1] < float(uniq), column, -1.0)
    row_ref[...] = jnp.broadcast_to(column, (padded, lane)).T[0:1].astype(i32)
    whole = jnp.maximum(ranks, 0.0).astype(i32)
    both = jnp.concatenate(
        [jnp.right_shift(whole, 4), jnp.bitwise_and(whole, 15)], axis=0
    ).astype(f32).astype(bf16)
    owner_at = lax.broadcasted_iota(i32, (groups, bags), 0)
    named = jnp.full((groups, bags), -1, i32)
    weight = jnp.zeros((groups, bags), f32)
    for slot in range(bag_len):
        got = jnp.dot(both, lows[slot], preferred_element_type=f32)
        pick = jnp.right_shift(loc_ref[slot : slot + 1, :], 7) == high_at
        big = jnp.sum(jnp.where(pick, got[:highs], 0.0), axis=0, keepdims=True)
        small = jnp.sum(jnp.where(pick, got[highs:], 0.0), axis=0, keepdims=True)
        pos = (16.0 * big + small).astype(i32)
        hit = own_ref[slot : slot + 1, :] == owner_at
        named = jnp.where(hit, pos, named)
        weight = jnp.where(hit, w_ref[slot : slot + 1, :], weight)
    pos_ref[...] = named
    wo_ref[...] = weight


def greet(axis, count, peer_of):
    barrier = pltpu.get_barrier_semaphore()

    def hello(k, _):
        pl.semaphore_signal(
            barrier, inc=1, device_id={axis: peer_of(k)}, device_id_type=MESH
        )
        return 0

    lax.fori_loop(1, count, hello, 0)


def gather_body(
    groups, fields, row_ref, table_ref, pos_ref, wo_ref, in_ref, rows_ref, lists_ref,
    wide, found, acc, list_send, list_recv, send_sem, recv_sem
):
    me = lax.axis_index("owner")
    samples = in_ref.shape[0]
    width = table_ref.shape[1]
    _, half, _ = rows_ref.shape
    padded = row_ref.shape[1]
    depth = table_ref.shape[0] // folds
    greet("owner", groups, lambda k: partner(me, k, groups))
    for j in range(folds):
        wide[:, j * width : (j + 1) * width] = table_ref[j * depth : (j + 1) * depth, :].astype(bf16)
    lists_ref[0] = row_ref[...]
    acc[...] = jnp.zeros_like(acc)
    pl.semaphore_wait(pltpu.get_barrier_semaphore(), groups - 1)

    def list_copy(k):
        return pltpu.make_async_remote_copy(
            src_ref=row_ref,
            dst_ref=lists_ref.at[k],
            send_sem=list_send.at[k],
            recv_sem=list_recv.at[k],
            device_id={"owner": partner(me, k, groups)},
            device_id_type=MESH,
        )

    def row_copy(k):
        return pltpu.make_async_remote_copy(
            src_ref=found.at[k],
            dst_ref=rows_ref.at[k],
            send_sem=send_sem.at[k],
            recv_sem=recv_sem.at[k],
            device_id={"owner": partner(me, k, groups)},
            device_id_type=MESH,
        )

    def send_list(i, _):
        list_copy(far_first(i, groups)).start()
        return 0

    lax.fori_loop(0, groups - 1, send_list, 0)
    lane_at = lax.broadcasted_iota(i32, (2 * half, lane), 1)

    def look(k):
        ids = jnp.broadcast_to(lists_ref[k], (lane, padded)).T[: 2 * half]
        within = ids
        for j in range(1, folds):
            within = jnp.where(ids >= j * depth, ids - j * depth, within)
        pick = jnp.concatenate(
            [
                jnp.where(within - c * lane == lane_at, 1.0, 0.0).astype(bf16)
                for c in range(depth // lane)
            ],
            axis=1,
        )
        every = jnp.dot(pick, wide[...], preferred_element_type=f32)
        row = every[:, :width]
        for j in range(1, folds):
            row = jnp.where(ids >= j * depth, every[:, j * width : (j + 1) * width], row)
        row = row.astype(bf16)
        return jnp.concatenate([row[:half], row[half:]], axis=1)

    def serve(i, _):
        k = far_first(i, groups)
        list_copy(k).wait_recv()
        found[k] = look(k)
        row_copy(k).start()
        return 0

    lax.fori_loop(0, groups - 1, serve, 0)
    rows_ref[0] = look(0)
    place = lax.broadcasted_iota(i32, (half, samples), 0)

    def pool(k):
        table_t = rows_ref[k].T
        for f in range(fields):
            at = slice(f * samples, (f + 1) * samples)
            pos = pos_ref[pl.ds(k, 1), at]
            upper = pos >= half
            pos = jnp.where(upper, pos - half, pos)
            mix = jnp.where(pos == place, wo_ref[pl.ds(k, 1), at], 0.0).astype(bf16)
            both = jnp.dot(table_t, mix, preferred_element_type=f32)
            rows = slice(f * width, (f + 1) * width)
            acc[rows, :] += jnp.where(upper, both[width:], both[:width])

    pool(0)

    def take(k, _):
        row_copy(k).wait_recv()
        pool(k)
        return 0

    lax.fori_loop(1, groups, take, 0)
    total = jnp.sum(wo_ref[...], axis=0, keepdims=True)
    for f in range(fields):
        pooled = acc[f * width : (f + 1) * width, :] / total[:, f * samples : (f + 1) * samples]
        in_ref[:, f * width : (f + 1) * width] = pooled.T.astype(bf16)

    def finish(k, _):
        list_copy(k).wait_send()
        row_copy(k).wait_send()
        return 0

    lax.fori_loop(1, groups, finish, 0)


def head_body(pieces, block, x_ref, label_ref, *refs):
    w_refs, b_refs, o_refs = refs[:pieces], refs[pieces : 2 * pieces], refs[2 * pieces : 3 * pieces]
    out_ref, w_all, pre, sems = refs[3 * pieces :]
    samples = x_ref.shape[0]
    plan = []
    for p in range(pieces):
        for c in range(0, w_refs[p].shape[1], block):
            plan.append((p, c))
    copies = []
    for i, (p, c) in enumerate(plan):
        copy = pltpu.make_async_copy(
            w_refs[p].at[:, pl.ds(c, block)], w_all.at[i], sems.at[i]
        )
        copy.start()
        copies.append(copy)
    part = jnp.zeros((samples, lane), f32)
    for i, (p, c) in enumerate(plan):
        copies[i].wait()
        bias = b_refs[p][:, c : c + block].astype(f32)
        out = o_refs[p][:, c : c + block].astype(f32)
        v = jnp.dot(x_ref[...], w_all[i], preferred_element_type=f32) + bias
        pre[i] = v
        term = v * (0.5 + 0.5 * jnp.tanh(0.5 * v)) * out
        for t in range(block // lane):
            part += term[:, t * lane : (t + 1) * lane]
    logits = jnp.sum(part, axis=1, keepdims=True)
    grad = jax.nn.sigmoid(logits) - label_ref[...].astype(f32)
    for i, (p, c) in enumerate(plan):
        out = o_refs[p][:, c : c + block].astype(f32)
        v = pre[i]
        sigma = 0.5 + 0.5 * jnp.tanh(0.5 * v)
        slope = sigma * (1.0 + v * (1.0 - sigma))
        dhidden = (grad * out * slope).astype(bf16)
        term = lax.dot_general(
            w_all[i], dhidden, (((1,), (1,)), ((), ())), preferred_element_type=f32
        )
        if i == 0:
            out_ref[...] = term
        else:
            out_ref[...] += term


def scatter_body(
    groups, parts, fields, pos_ref, wo_ref, own_ref, w_ref, rows_ref, dp_ref, lists_ref,
    wg_ref, sums_ref, dp, scaled, along, mixes, dps, found, got, acc,
    send_sem, recv_sem, dense_send, dense_recv
):
    me = lax.axis_index("owner")
    lay = lax.axis_index("dense")
    bag_len, bags = own_ref.shape
    samples = bags // fields
    width = dp_ref.shape[0] // fields
    _, half, _ = rows_ref.shape
    padded = lists_ref.shape[2]
    depth = sums_ref.shape[1] // folds
    greet("owner", groups, lambda k: partner(me, k, groups))
    greet("dense", parts, lambda k: lax.rem(lay + k, parts))
    total = jnp.sum(w_ref[...], axis=0, keepdims=True)
    scaled[...] = wo_ref[...] / total
    along[...] = jnp.zeros_like(along)
    dp[...] = dp_ref[...].astype(bf16)
    acc[...] = jnp.zeros_like(acc)
    pl.semaphore_wait(pltpu.get_barrier_semaphore(), groups + parts - 2)

    def grad_copy(k):
        return pltpu.make_async_remote_copy(
            src_ref=found.at[k],
            dst_ref=got.at[k],
            send_sem=send_sem.at[k],
            recv_sem=recv_sem.at[k],
            device_id={"owner": partner(me, k, groups)},
            device_id_type=MESH,
        )

    def dense_copy(k, j):
        return pltpu.make_async_remote_copy(
            src_ref=sums_ref.at[lay, pl.ds(j * depth, depth)],
            dst_ref=sums_ref.at[lay, pl.ds(j * depth, depth)],
            send_sem=dense_send.at[k, j],
            recv_sem=dense_recv.at[k, j],
            device_id={"dense": lax.rem(lay + k, parts)},
            device_id_type=MESH,
        )

    place = lax.broadcasted_iota(i32, (half, samples), 0)

    def grads(k):
        for f in range(fields):
            at = slice(f * samples, (f + 1) * samples)
            pos = pos_ref[pl.ds(k, 1), at]
            upper = pos >= half
            pos = jnp.where(upper, pos - half, pos)
            hit = pos == place
            mixes[:, at] = jnp.where(hit, scaled[pl.ds(k, 1), at], 0.0).astype(bf16)
            field = dp[f * width : (f + 1) * width, :]
            high = field * jnp.where(upper, 1.0, 0.0).astype(bf16)
            both = jnp.concatenate([field - high, high], axis=0)
            dps[:, at] = both
            dots = jnp.dot(rows_ref[k], both, preferred_element_type=f32)
            mine = jnp.sum(jnp.where(hit, dots, 0.0), axis=0, keepdims=True)
            along[:, at] += jnp.where(own_ref[:, at] == k, mine, 0.0)
        sums = lax.dot_general(
            dps[...], mixes[...], (((1,), (1,)), ((), ())), preferred_element_type=f32
        )
        return sums.T.astype(bf16)

    def give(i, _):
        k = far_first(i, groups)
        found[k] = grads(k)
        grad_copy(k).start()
        return 0

    lax.fori_loop(0, groups - 1, give, 0)
    got[0] = grads(0)
    centre = jnp.sum(w_ref[...] * along[...], axis=0, keepdims=True) / total
    wg_ref[...] = (along[...] - centre) / total
    deep = lax.broadcasted_iota(i32, (depth, 2 * half), 0)

    def collect(k):
        row = lists_ref[k]
        ids = jnp.broadcast_to(row, (lane, padded)).T[: 2 * half]
        row = row[:, : 2 * half]
        within = row
        for j in range(1, folds):
            within = jnp.where(row >= j * depth, row - j * depth, within)
        pick = jnp.where(within == deep, 1.0, 0.0).astype(bf16)
        here = got[k].astype(f32)
        here = jnp.concatenate([here[:, :width], here[:, width:]], axis=0)
        split = jnp.concatenate(
            [
                jnp.where((ids >= j * depth) & (ids < (j + 1) * depth), here, 0.0).astype(bf16)
                for j in range(folds)
            ],
            axis=1,
        )
        acc[...] += jnp.dot(pick, split, preferred_element_type=f32)

    collect(0)

    def take(k, _):
        grad_copy(k).wait_recv()
        collect(k)
        return 0

    lax.fori_loop(1, groups, take, 0)
    for j in range(folds):
        sums_ref[lay, j * depth : (j + 1) * depth, :] = acc[:, j * width : (j + 1) * width].astype(bf16)
        for k in range(1, parts):
            dense_copy(k, j).start()

    def finish(k, _):
        grad_copy(k).wait_send()
        return 0

    lax.fori_loop(1, groups, finish, 0)
    for k in range(1, parts):
        for j in range(folds):
            dense_copy(k, j).wait()


def send_weights(w_in, b_in, w_out):
    parts = lax.axis_size("dense")
    half = w_in.shape[1] // 2
    core = lax.rem(lax.axis_index("owner"), 2)
    mine = lax.dynamic_slice_in_dim(w_in, core * half, half, axis=1)
    arrived = []
    for shift in range(1, parts):
        ring = [(d, (d + shift) % parts) for d in range(parts)]
        arrived.append(tuple(lax.ppermute(x, "dense", ring) for x in (mine, b_in, w_out)))
    return arrived


def head_pieces(w_in, b_in, w_out, arrived):
    groups = lax.axis_size("owner")
    half = w_in.shape[1] // 2
    core = lax.rem(lax.axis_index("owner"), 2)
    swap = [(g, g + 1 - 2 * (g % 2)) for g in range(groups)]
    pieces = [(w_in, b_in, w_out)]
    for w_here, b_all, o_all in arrived:
        w_there = lax.ppermute(w_here, "owner", swap)
        for w_piece, at in ((w_here, core * half), (w_there, (1 - core) * half)):
            pieces.append(
                (
                    w_piece,
                    lax.dynamic_slice_in_dim(b_all, at, half),
                    lax.dynamic_slice_in_dim(o_all, at, half),
                )
            )
    return pieces


def head(inputs, labels, pieces):
    samples, wide = inputs.shape
    block = 512
    count = sum(w.shape[1] for w, _, _ in pieces) // block
    hbm = pl.BlockSpec(memory_space=pl.ANY)
    n = len(pieces)
    return pl.pallas_call(
        functools.partial(head_body, n, block),
        out_shape=jax.ShapeDtypeStruct((wide, samples), f32),
        in_specs=[vmem(), vmem()] + [hbm] * n + [vmem()] * (2 * n),
        out_specs=vmem(),
        scratch_shapes=[
            pltpu.VMEM((count, wide, block), bf16),
            pltpu.VMEM((count, samples, block), f32),
            pltpu.SemaphoreType.DMA((count,)),
        ],
        compiler_params=pltpu.CompilerParams(vmem_limit_bytes=room),
        name="head",
    )(
        inputs,
        labels[:, None],
        *[w for w, _, _ in pieces],
        *[b[None, :] for _, b, _ in pieces],
        *[o[None, :] for _, _, o in pieces],
    )


def local(owners, local_rows, weights, labels, table, accum, w_in, b_in, w_out):
    samples, fields, bag_len = owners.shape
    table_rows, width = table.shape
    groups = lax.axis_size("owner")
    parts = lax.axis_size("dense")
    bags = samples * fields
    uniq = bags * bag_len // (2 * groups)
    half = -(-uniq // 32) * 16
    padded = -(-2 * half // lane) * lane
    depth = table_rows // folds
    arrived = send_weights(w_in, b_in, w_out)

    def by_slot(x):
        return x.transpose(2, 1, 0).reshape(bag_len, bags)

    own, loc, w = by_slot(owners ^ lax.axis_index("owner")), by_slot(local_rows), by_slot(weights)
    distinct, pos, spread = pl.pallas_call(
        functools.partial(distinct_body, table_rows, uniq),
        out_shape=(
            jax.ShapeDtypeStruct((1, padded), i32),
            jax.ShapeDtypeStruct((groups, bags), i32),
            jax.ShapeDtypeStruct((groups, bags), f32),
        ),
        in_specs=[vmem()] * 3,
        out_specs=(vmem(),) * 3,
        scratch_shapes=[pltpu.VMEM((bag_len, lane, bags), bf16)],
        compiler_params=pltpu.CompilerParams(vmem_limit_bytes=room),
        name="distinct",
    )(own, loc, w)
    dma = pltpu.SemaphoreType.DMA
    inputs, rows, lists = pl.pallas_call(
        functools.partial(gather_body, groups, fields),
        out_shape=(
            jax.ShapeDtypeStruct((samples, fields * width), bf16),
            jax.ShapeDtypeStruct((groups, half, 2 * width), bf16),
            jax.ShapeDtypeStruct((groups, 1, padded), i32),
        ),
        in_specs=[vmem()] * 4,
        out_specs=(vmem(),) * 3,
        scratch_shapes=[
            pltpu.VMEM((depth, folds * width), bf16),
            pltpu.VMEM((groups, half, 2 * width), bf16),
            pltpu.VMEM((fields * width, samples), f32),
            dma((groups,)),
            dma((groups,)),
            dma((groups,)),
            dma((groups,)),
        ],
        compiler_params=pltpu.CompilerParams(
            collective_id=0, has_side_effects=True, vmem_limit_bytes=room
        ),
        name="gather",
    )(distinct, table, pos, spread)

    inputs, arrived = lax.optimization_barrier((inputs, arrived))
    pieces = head_pieces(w_in, b_in, w_out, arrived)
    dinputs = head(inputs, labels, pieces)

    weight_grad, sums = pl.pallas_call(
        functools.partial(scatter_body, groups, parts, fields),
        out_shape=(
            jax.ShapeDtypeStruct((bag_len, bags), f32),
            jax.ShapeDtypeStruct((parts, table_rows, width), bf16),
        ),
        in_specs=[vmem()] * 7,
        out_specs=(vmem(),) * 2,
        scratch_shapes=[
            pltpu.VMEM((fields * width, samples), bf16),
            pltpu.VMEM((groups, bags), f32),
            pltpu.VMEM((bag_len, bags), f32),
            pltpu.VMEM((half, bags), bf16),
            pltpu.VMEM((2 * width, bags), bf16),
            pltpu.VMEM((groups, half, 2 * width), bf16),
            pltpu.VMEM((groups, half, 2 * width), bf16),
            pltpu.VMEM((depth, folds * width), f32),
            dma((groups,)),
            dma((groups,)),
            dma((parts, folds)),
            dma((parts, folds)),
        ],
        compiler_params=pltpu.CompilerParams(
            collective_id=1, has_side_effects=True, vmem_limit_bytes=room
        ),
        name="scatter",
    )(pos, spread, own, w, rows, dinputs, lists)
    weight_grad = weight_grad.reshape(bag_len, fields, samples).transpose(2, 1, 0)
    row_grad = jnp.sum(sums.astype(f32), axis=0)
    new_accum = accum + jnp.mean(row_grad * row_grad, axis=-1)
    new_table = table - step_size * row_grad / jnp.sqrt(new_accum)[:, None]
    return (new_table, new_accum, weight_grad)


def solution(mesh):
    placed = (
        P(("owner", "dense"), None, None),
        P(("owner", "dense"), None, None),
        P(("owner", "dense"), None, None),
        P(("owner", "dense")),
        P("owner", None),
        P("owner"),
        P(None, "dense"),
        P("dense"),
        P("dense"),
    )
    return jax.shard_map(
        local,
        mesh=mesh,
        in_specs=placed,
        out_specs=(P("owner", None), P("owner"), P(("owner", "dense"), None, None)),
        check_vma=False,
    )
```

```python
import functools

import jax
import jax.numpy as jnp
from jax import lax
from jax.experimental import pallas as pl
from jax.experimental.pallas import tpu as pltpu
from jax.sharding import PartitionSpec as P

step_size = 0.5
lane = 128
folds = 4
slab = 64
f32 = jnp.float32
bf16 = jnp.bfloat16
i32 = jnp.int32
MESH = pl.DeviceIdType.MESH
room = 48 * 1024 * 1024


def vmem():
    return pl.BlockSpec(memory_space=pltpu.VMEM)


def partner(me, k, groups):
    peer = me
    bit = 1
    while bit < groups:
        flip = lax.rem(lax.div(k, bit), 2)
        peer = peer + bit * flip * (1 - 2 * lax.rem(lax.div(me, bit), 2))
        bit *= 2
    return peer


def far_first(i, groups):
    half = groups // 2
    return lax.rem(i + half, groups) + lax.div(i, half)


def in_turn(i, groups):
    odd = lax.rem(i, 2)
    return odd + lax.div(i, 2) + (1 - odd) * (groups // 2)


def name_rows(table_rows, uniq, own_ref, loc_ref, w_ref, row_ref, pos_ref, wo_ref, lows):
    bag_len, bags = own_ref.shape
    groups = pos_ref.shape[0]
    padded = row_ref.shape[1]
    highs = table_rows // lane
    counts = jnp.zeros((highs, lane), f32)
    low_at = lax.broadcasted_iota(i32, (lane, bags), 0)
    high_at = lax.broadcasted_iota(i32, (highs, bags), 0)
    for slot in range(bag_len):
        loc = loc_ref[slot : slot + 1, :]
        low = jnp.where(jnp.bitwise_and(loc, lane - 1) == low_at, 1.0, 0.0).astype(bf16)
        lows[slot] = low
        high = jnp.where(jnp.right_shift(loc, 7) == high_at, 1.0, 0.0).astype(bf16)
        counts += lax.dot_general(high, low, (((1,), (1,)), ((), ())), preferred_element_type=f32)
    present = jnp.where(counts > 0.0, 1.0, 0.0)
    upper = jnp.where(
        lax.broadcasted_iota(i32, (lane, lane), 0) <= lax.broadcasted_iota(i32, (lane, lane), 1),
        1.0,
        0.0,
    ).astype(bf16)
    below = jnp.where(
        lax.broadcasted_iota(i32, (highs, highs), 0) > lax.broadcasted_iota(i32, (highs, highs), 1),
        1.0,
        0.0,
    ).astype(bf16)
    inclusive = jnp.dot(present.astype(bf16), upper, preferred_element_type=f32)
    before = jnp.sum(
        jnp.dot(below, present.astype(bf16), preferred_element_type=f32), axis=1, keepdims=True
    )
    ranks = jnp.where(present > 0.0, inclusive + before - 1.0, -1.0)
    place = lax.broadcasted_iota(i32, (padded, lane), 0).astype(f32)
    lane_at = lax.broadcasted_iota(i32, (1, lane), 1).astype(f32)
    found = jnp.where(place < float(uniq), 0.0, -1.0)
    for h in range(highs):
        found += jnp.where(place == ranks[h : h + 1, :], lane_at + float(h * lane), 0.0)
    column = jnp.sum(found, axis=1, keepdims=True)
    column = jnp.where(place[:, :1] < float(uniq), column, -1.0)
    row_ref[...] = jnp.broadcast_to(column, (padded, lane)).T[0:1].astype(i32)
    whole = jnp.maximum(ranks, 0.0).astype(i32)
    both = jnp.concatenate(
        [jnp.right_shift(whole, 4), jnp.bitwise_and(whole, 15)], axis=0
    ).astype(f32).astype(bf16)
    owner_at = lax.broadcasted_iota(i32, (groups, bags), 0)
    named = jnp.full((groups, bags), -1, i32)
    weight = jnp.zeros((groups, bags), f32)
    for slot in range(bag_len):
        got = jnp.dot(both, lows[slot], preferred_element_type=f32)
        pick = jnp.right_shift(loc_ref[slot : slot + 1, :], 7) == high_at
        big = jnp.sum(jnp.where(pick, got[:highs], 0.0), axis=0, keepdims=True)
        small = jnp.sum(jnp.where(pick, got[highs:], 0.0), axis=0, keepdims=True)
        pos = (16.0 * big + small).astype(i32)
        hit = own_ref[slot : slot + 1, :] == owner_at
        named = jnp.where(hit, pos, named)
        weight = jnp.where(hit, w_ref[slot : slot + 1, :], weight)
    pos_ref[...] = named
    wo_ref[...] = weight


def greet(axis, count, peer_of):
    barrier = pltpu.get_barrier_semaphore()

    def hello(k, _):
        pl.semaphore_signal(
            barrier, inc=1, device_id={axis: peer_of(k)}, device_id_type=MESH
        )
        return 0

    lax.fori_loop(1, count, hello, 0)


def gather_body(
    groups, parts, fields, uniq, own_hbm, loc_hbm, w_hbm, table_hbm, win_ref, b_ref, o_ref,
    in_ref, rows_ref, lists_ref, pos_ref, wo_ref, own_ref, wot_ref, bt_ref, ot_ref,
    row, loc_ref, w_ref, table_ref, in_sems, lows, wide, found, acc, list_send, list_recv, send_sem, recv_sem,
    bo_send, bo_recv, y_send, y_recv, x_send, x_recv, s_send, s_recv, t_send, t_recv
):
    me = lax.axis_index("owner")
    lay = lax.axis_index("dense")
    samples = in_ref.shape[0]
    table_rows, width = table_ref.shape
    _, half, _ = rows_ref.shape
    padded = row.shape[1]
    depth = table_rows // folds
    greet("dense", parts, lambda k: lax.rem(lay + k, parts))
    greet("owner", groups, lambda k: partner(me, k, groups))
    loads = []
    for i, (source, target) in enumerate(
        ((loc_hbm, loc_ref), (own_hbm, own_ref), (w_hbm, w_ref), (table_hbm, table_ref))
    ):
        loads.append(pltpu.make_async_copy(source, target, in_sems.at[i]))
        loads[i].start()
    pl.semaphore_wait(pltpu.get_barrier_semaphore(), groups + parts - 2)

    slabs = win_ref.shape[0] // slab
    passed = slabs // 5
    direct = slabs // 2 - passed
    core = lax.rem(me, 2)
    side = lax.rem(lax.div(me, 2), 2)

    def slab_of(its_side, its_core, i):
        j = 2 * i + its_core
        j = j + its_side * (slabs - 1 - 2 * j)
        return pl.ds(pl.multiple_of(j * slab, slab), slab)

    def y_copy(s, i):
        at = slab_of(side, core, i)
        return pltpu.make_async_remote_copy(
            src_ref=win_ref.at[at],
            dst_ref=wot_ref.at[s - 1, at],
            send_sem=y_send.at[s - 1, i],
            recv_sem=y_recv.at[s - 1, i],
            device_id={"dense": lax.rem(lay + s, parts)},
            device_id_type=MESH,
        )

    def pass_on(s, at, i, k, send, recv):
        return pltpu.make_async_remote_copy(
            src_ref=wot_ref.at[s - 1, at],
            dst_ref=wot_ref.at[s - 1, at],
            send_sem=send.at[s - 1, i],
            recv_sem=recv.at[s - 1, i],
            device_id={"owner": partner(me, k, groups)},
            device_id_type=MESH,
        )

    def x_copy(s, i):
        return pass_on(s, slab_of(side, core, i), i, 2, x_send, x_recv)

    def s_copy(s, i):
        return pass_on(s, slab_of(side, core, i), i, 1, s_send, s_recv)

    def t_copy(s, i):
        return pass_on(s, slab_of(1 - side, core, i), i, 1, t_send, t_recv)

    def each_layer(act):
        for s in range(1, parts):
            act(s)

    def bo_copies(s):
        return [
            pltpu.make_async_remote_copy(
                src_ref=source,
                dst_ref=target.at[s - 1],
                send_sem=bo_send.at[s - 1, i],
                recv_sem=bo_recv.at[s - 1, i],
                device_id={"dense": lax.rem(lay + s, parts)},
                device_id_type=MESH,
            )
            for i, (source, target) in enumerate(((b_ref, bt_ref), (o_ref, ot_ref)))
        ]

    def start_y(i, _):
        each_layer(lambda s: y_copy(s, i).start())
        return 0

    first = passed // 2
    second = 2 * first
    lax.fori_loop(0, first, start_y, 0)
    each_layer(lambda s: [copy.start() for copy in bo_copies(s)])

    def y_in(i, _):
        def act(s):
            y_copy(s, i).wait_recv()
            s_copy(s, i).start()

            @pl.when(i < passed)
            def _():
                x_copy(s, i).start()

        each_layer(act)
        return 0

    def x_in(i, _):
        def act(s):
            x_copy(s, i).wait_recv()
            t_copy(s, i).start()

        each_layer(act)
        return 0

    for load in loads[:3]:
        load.wait()
    own_ref[...] = jnp.bitwise_xor(own_ref[...], me)
    name_rows(table_rows, uniq, own_ref, loc_ref, w_ref, row, pos_ref, wo_ref, lows)
    lists_ref[0] = row[...]

    def list_copy(k):
        return pltpu.make_async_remote_copy(
            src_ref=row,
            dst_ref=lists_ref.at[k],
            send_sem=list_send.at[k],
            recv_sem=list_recv.at[k],
            device_id={"owner": partner(me, k, groups)},
            device_id_type=MESH,
        )

    def row_copy(k):
        return pltpu.make_async_remote_copy(
            src_ref=found.at[k],
            dst_ref=rows_ref.at[k],
            send_sem=send_sem.at[k],
            recv_sem=recv_sem.at[k],
            device_id={"owner": partner(me, k, groups)},
            device_id_type=MESH,
        )

    def send_list(i, _):
        list_copy(far_first(i, groups)).start()
        return 0

    lax.fori_loop(0, groups - 1, send_list, 0)
    loads[3].wait()
    for j in range(folds):
        wide[:, j * width : (j + 1) * width] = table_ref[j * depth : (j + 1) * depth, :].astype(bf16)
    lane_at = lax.broadcasted_iota(i32, (2 * half, lane), 1)

    def look(k):
        ids = jnp.broadcast_to(lists_ref[k], (lane, padded)).T[: 2 * half]
        within = ids
        for j in range(1, folds):
            within = jnp.where(ids >= j * depth, ids - j * depth, within)
        pick = jnp.concatenate(
            [
                jnp.where(within - c * lane == lane_at, 1.0, 0.0).astype(bf16)
                for c in range(depth // lane)
            ],
            axis=1,
        )
        every = jnp.dot(pick, wide[...], preferred_element_type=f32)
        one = every[:, :width]
        for j in range(1, folds):
            one = jnp.where(ids >= j * depth, every[:, j * width : (j + 1) * width], one)
        one = one.astype(bf16)
        return jnp.concatenate([one[:half], one[half:]], axis=1)

    def serve(i, _):
        k = far_first(i, groups)
        list_copy(k).wait_recv()
        found[k] = look(k)
        row_copy(k).start()
        return 0

    lax.fori_loop(0, groups // 2, serve, 0)
    lax.fori_loop(first, second, start_y, 0)
    lax.fori_loop(groups // 2, groups - 1, serve, 0)
    rows_ref[0] = look(0)
    place = lax.broadcasted_iota(i32, (half, samples), 0)

    def pool(k):
        table_t = rows_ref[k].T
        for f in range(fields):
            at = slice(f * samples, (f + 1) * samples)
            pos = pos_ref[pl.ds(k, 1), at]
            upper = pos >= half
            pos = jnp.where(upper, pos - half, pos)
            mix = jnp.where(pos == place, wo_ref[pl.ds(k, 1), at], 0.0).astype(bf16)
            both = jnp.dot(table_t, mix, preferred_element_type=f32)
            rows = slice(f * width, (f + 1) * width)
            acc[rows, :] += jnp.where(upper, both[width:], both[:width])

    near = groups // 2
    lax.fori_loop(0, first, y_in, 0)
    lax.fori_loop(second, passed, start_y, 0)
    acc[...] = jnp.zeros_like(acc)

    def take_near(k, _):
        @pl.when(k > 0)
        def _():
            row_copy(k).wait_recv()

        pool(k)
        return 0

    lax.fori_loop(0, near, take_near, 0)
    lax.fori_loop(first, second, y_in, 0)
    lax.fori_loop(passed, direct, start_y, 0)
    lax.fori_loop(second, passed, y_in, 0)

    def take_far(j, _):
        row_copy(near + j).wait_recv()
        pool(near + j)
        return 0

    lax.fori_loop(0, near // 2, take_far, 0)
    lax.fori_loop(0, first, x_in, 0)
    lax.fori_loop(near // 2, near, take_far, 0)
    lax.fori_loop(first, passed, x_in, 0)
    lax.fori_loop(passed, direct, y_in, 0)
    total = jnp.sum(wo_ref[...], axis=0, keepdims=True)
    for f in range(fields):
        pooled = acc[f * width : (f + 1) * width, :] / total[:, f * samples : (f + 1) * samples]
        in_ref[:, f * width : (f + 1) * width] = pooled.T.astype(bf16)

    def finish(k, _):
        list_copy(k).wait_send()
        row_copy(k).wait_send()
        return 0

    lax.fori_loop(1, groups, finish, 0)
    each_layer(lambda s: [copy.wait() for copy in bo_copies(s)])

    def y_out(i, _):
        def act(s):
            y_copy(s, i).wait_send()
            s_copy(s, i).wait()

        each_layer(act)
        return 0

    def x_out(i, _):
        def act(s):
            x_copy(s, i).wait_send()
            t_copy(s, i).wait()

        each_layer(act)
        return 0

    lax.fori_loop(0, direct, y_out, 0)
    lax.fori_loop(0, passed, x_out, 0)


def head_body(
    parts, block, x_ref, label_ref, w_ref, b_ref, o_ref, wot_ref, bt_ref, ot_ref,
    out_ref, w_all, pre, sems
):
    samples = x_ref.shape[0]
    plan = [(p, c) for p in range(parts) for c in range(0, w_ref.shape[1], block)]
    copies = []
    for i, (p, c) in enumerate(plan):
        source = w_ref if p == 0 else wot_ref.at[p - 1]
        copy = pltpu.make_async_copy(source.at[:, pl.ds(c, block)], w_all.at[i], sems.at[i])
        copy.start()
        copies.append(copy)

    def spread(lines, c):
        return jnp.concatenate(
            [lines[r : r + 1] for r in range(c // lane, (c + block) // lane)], axis=1
        )

    biases = [b_ref[...].astype(f32)] + [bt_ref[p].astype(f32) for p in range(parts - 1)]
    outs = [o_ref[...].astype(f32)] + [ot_ref[p].astype(f32) for p in range(parts - 1)]
    part = jnp.zeros((samples, lane), f32)
    for i, (p, c) in enumerate(plan):
        copies[i].wait()
        bias, out = spread(biases[p], c), spread(outs[p], c)
        v = jnp.dot(x_ref[...], w_all[i], preferred_element_type=f32) + bias
        pre[i] = v
        term = v * (0.5 + 0.5 * jnp.tanh(0.5 * v)) * out
        for t in range(block // lane):
            part += term[:, t * lane : (t + 1) * lane]
    logits = jnp.sum(part, axis=1, keepdims=True)
    label = label_ref[...].astype(f32)
    label = jnp.concatenate(
        [
            jnp.broadcast_to(label[r : r + 1], (lane, lane)).T[:, :1]
            for r in range(samples // lane)
        ],
        axis=0,
    )
    grad = jax.nn.sigmoid(logits) - label
    for i, (p, c) in enumerate(plan):
        out = spread(outs[p], c)
        v = pre[i]
        sigma = 0.5 + 0.5 * jnp.tanh(0.5 * v)
        slope = sigma * (1.0 + v * (1.0 - sigma))
        dhidden = (grad * out * slope).astype(bf16)
        term = lax.dot_general(
            w_all[i], dhidden, (((1,), (1,)), ((), ())), preferred_element_type=f32
        )
        if i == 0:
            out_ref[...] = term
        else:
            out_ref[...] += term


def scatter_body(
    groups, parts, fields, pos_ref, wo_ref, own_ref, w_ref, rows_ref, dp_ref, lists_ref,
    table_ref, accum_ref, wg_ref, new_table_ref, new_accum_ref, sums_ref, dp, scaled, along, mixes, dps, found, got, acc,
    send_sem, recv_sem, dense_send, dense_recv
):
    me = lax.axis_index("owner")
    lay = lax.axis_index("dense")
    bag_len, bags = own_ref.shape
    samples = bags // fields
    width = dp_ref.shape[0] // fields
    _, half, _ = rows_ref.shape
    padded = lists_ref.shape[2]
    depth = sums_ref.shape[1] // folds
    greet("owner", groups, lambda k: partner(me, k, groups))
    greet("dense", parts, lambda k: lax.rem(lay + k, parts))
    total = jnp.sum(w_ref[...], axis=0, keepdims=True)
    scaled[...] = wo_ref[...] / total
    along[...] = jnp.zeros_like(along)
    dp[...] = dp_ref[...].astype(bf16)
    acc[...] = jnp.zeros_like(acc)
    pl.semaphore_wait(pltpu.get_barrier_semaphore(), groups + parts - 2)

    def grad_copy(k):
        return pltpu.make_async_remote_copy(
            src_ref=found.at[k],
            dst_ref=got.at[k],
            send_sem=send_sem.at[k],
            recv_sem=recv_sem.at[k],
            device_id={"owner": partner(me, k, groups)},
            device_id_type=MESH,
        )

    def dense_copy(k, j):
        return pltpu.make_async_remote_copy(
            src_ref=sums_ref.at[lay, pl.ds(j * depth, depth)],
            dst_ref=sums_ref.at[lay, pl.ds(j * depth, depth)],
            send_sem=dense_send.at[k, j],
            recv_sem=dense_recv.at[k, j],
            device_id={"dense": lax.rem(lay + k, parts)},
            device_id_type=MESH,
        )

    place = lax.broadcasted_iota(i32, (half, samples), 0)

    def grads(k):
        for f in range(fields):
            at = slice(f * samples, (f + 1) * samples)
            pos = pos_ref[pl.ds(k, 1), at]
            upper = pos >= half
            pos = jnp.where(upper, pos - half, pos)
            hit = pos == place
            mixes[:, at] = jnp.where(hit, scaled[pl.ds(k, 1), at], 0.0).astype(bf16)
            field = dp[f * width : (f + 1) * width, :]
            high = field * jnp.where(upper, 1.0, 0.0).astype(bf16)
            both = jnp.concatenate([field - high, high], axis=0)
            dps[:, at] = both
            dots = jnp.dot(rows_ref[k], both, preferred_element_type=f32)
            mine = jnp.sum(jnp.where(hit, dots, 0.0), axis=0, keepdims=True)
            along[:, at] += jnp.where(own_ref[:, at] == k, mine, 0.0)
        sums = lax.dot_general(
            dps[...], mixes[...], (((1,), (1,)), ((), ())), preferred_element_type=f32
        )
        return sums.T.astype(bf16)

    def give(i, _):
        k = in_turn(i, groups)
        found[k] = grads(k)
        grad_copy(k).start()
        return 0

    lax.fori_loop(0, groups - 1, give, 0)
    got[0] = grads(0)
    centre = jnp.sum(w_ref[...] * along[...], axis=0, keepdims=True) / total
    for f in range(fields):
        at = slice(f * samples, (f + 1) * samples)
        wg_ref[f] = (along[:, at] - centre[:, at]) / total[:, at]
    deep = lax.broadcasted_iota(i32, (depth, 2 * half), 0)

    def collect(k):
        row = lists_ref[k]
        ids = jnp.broadcast_to(row, (lane, padded)).T[: 2 * half]
        row = row[:, : 2 * half]
        within = row
        for j in range(1, folds):
            within = jnp.where(row >= j * depth, row - j * depth, within)
        pick = jnp.where(within == deep, 1.0, 0.0).astype(bf16)
        here = got[k].astype(f32)
        here = jnp.concatenate([here[:, :width], here[:, width:]], axis=0)
        split = jnp.concatenate(
            [
                jnp.where((ids >= j * depth) & (ids < (j + 1) * depth), here, 0.0).astype(bf16)
                for j in range(folds)
            ],
            axis=1,
        )
        acc[...] += jnp.dot(pick, split, preferred_element_type=f32)

    collect(0)

    def take(k, _):
        grad_copy(k).wait_recv()
        collect(k)
        return 0

    lax.fori_loop(1, groups, take, 0)
    for j in range(folds):
        sums_ref[lay, j * depth : (j + 1) * depth, :] = acc[:, j * width : (j + 1) * width].astype(bf16)
        for k in range(1, parts):
            dense_copy(k, j).start()

    rows_of = depth // lane
    for j in range(folds):
        for k in range(1, parts):
            dense_copy(k, j).wait_recv()
        for c in range(j * rows_of, (j + 1) * rows_of):
            at = slice(c * lane, (c + 1) * lane)
            total_grad = sums_ref[0, at, :].astype(f32)
            for p in range(1, parts):
                total_grad += sums_ref[p, at, :].astype(f32)
            square = (total_grad * total_grad).T
            grown = accum_ref[c : c + 1, :] + jnp.sum(square, axis=0, keepdims=True) * (1.0 / width)
            new_accum_ref[c : c + 1, :] = grown
            scale = jnp.broadcast_to(step_size * lax.rsqrt(grown), (lane, lane)).T
            new_table_ref[at, :] = table_ref[at, :] - total_grad * scale

    def finish(k, _):
        grad_copy(k).wait_send()
        return 0

    lax.fori_loop(1, groups, finish, 0)
    for k in range(1, parts):
        for j in range(folds):
            dense_copy(k, j).wait_send()


def head(inputs, labels, w_in, bias, out_w, other_w, other_b, other_o):
    samples, wide = inputs.shape
    block = 512
    parts = lax.axis_size("dense")
    count = parts * w_in.shape[1] // block
    hbm = pl.BlockSpec(memory_space=pltpu.HBM)
    return pl.pallas_call(
        functools.partial(head_body, parts, block),
        out_shape=jax.ShapeDtypeStruct((wide, samples), f32),
        in_specs=[vmem(), vmem(), hbm, vmem(), vmem(), hbm, vmem(), vmem()],
        out_specs=vmem(),
        scratch_shapes=[
            pltpu.VMEM((count, wide, block), bf16),
            pltpu.VMEM((count, samples, block), f32),
            pltpu.SemaphoreType.DMA((count,)),
        ],
        compiler_params=pltpu.CompilerParams(vmem_limit_bytes=room),
        name="head",
    )(inputs, labels.reshape(-1, lane), w_in, bias, out_w, other_w, other_b, other_o)


def local(owners, local_rows, weights, labels, table, accum, w_in, b_in, w_out):
    samples, fields, bag_len = owners.shape
    table_rows, width = table.shape
    groups = lax.axis_size("owner")
    parts = lax.axis_size("dense")
    bags = samples * fields
    uniq = bags * bag_len // (2 * groups)
    half = -(-uniq // 32) * 16
    padded = -(-2 * half // lane) * lane
    depth = table_rows // folds

    def by_slot(x):
        return x.transpose(2, 1, 0).reshape(bag_len, bags)

    own, loc, w = by_slot(owners), by_slot(local_rows), by_slot(weights)
    lines = w_in.shape[1] // lane
    bias, out_w = b_in.reshape(lines, lane), w_out.reshape(lines, lane)
    dma = pltpu.SemaphoreType.DMA
    hbm = pl.BlockSpec(memory_space=pltpu.HBM)
    wide, hidden = w_in.shape
    layers = parts - 1
    passed = wide // slab // 5
    direct = wide // slab // 2 - passed
    inputs, rows, lists, pos, spread, own, other_w, other_b, other_o = pl.pallas_call(
        functools.partial(gather_body, groups, parts, fields, uniq),
        out_shape=(
            jax.ShapeDtypeStruct((samples, fields * width), bf16),
            jax.ShapeDtypeStruct((groups, half, 2 * width), bf16),
            jax.ShapeDtypeStruct((groups, 1, padded), i32),
            jax.ShapeDtypeStruct((groups, bags), i32),
            jax.ShapeDtypeStruct((groups, bags), f32),
            jax.ShapeDtypeStruct((bag_len, bags), i32),
            jax.ShapeDtypeStruct((layers, wide, hidden), bf16),
            jax.ShapeDtypeStruct((layers, lines, lane), bf16),
            jax.ShapeDtypeStruct((layers, lines, lane), bf16),
        ),
        in_specs=[hbm] * 7,
        out_specs=(vmem(),) * 6 + (hbm, vmem(), vmem()),
        scratch_shapes=[
            pltpu.VMEM((1, padded), i32),
            pltpu.VMEM((bag_len, bags), i32),
            pltpu.VMEM((bag_len, bags), f32),
            pltpu.VMEM((table_rows, width), f32),
            dma((4,)),
            pltpu.VMEM((bag_len, lane, bags), bf16),
            pltpu.VMEM((depth, folds * width), bf16),
            pltpu.VMEM((groups, half, 2 * width), bf16),
            pltpu.VMEM((fields * width, samples), f32),
            dma((groups,)),
            dma((groups,)),
            dma((groups,)),
            dma((groups,)),
            dma((layers, 2)),
            dma((layers, 2)),
            dma((layers, direct)),
            dma((layers, direct)),
            dma((layers, passed)),
            dma((layers, passed)),
            dma((layers, direct)),
            dma((layers, direct)),
            dma((layers, passed)),
            dma((layers, passed)),
        ],
        compiler_params=pltpu.CompilerParams(
            collective_id=0, has_side_effects=True, vmem_limit_bytes=room
        ),
        name="gather",
    )(own, loc, w, table, w_in, bias, out_w)
    dinputs = head(inputs, labels, w_in, bias, out_w, other_w, other_b, other_o)

    weight_grad, new_table, new_accum = pl.pallas_call(
        functools.partial(scatter_body, groups, parts, fields),
        out_shape=(
            jax.ShapeDtypeStruct((fields, bag_len, samples), f32),
            jax.ShapeDtypeStruct((table_rows, width), f32),
            jax.ShapeDtypeStruct((table_rows // lane, lane), f32),
        ),
        in_specs=[vmem()] * 9,
        out_specs=(vmem(),) * 3,
        scratch_shapes=[
            pltpu.VMEM((parts, table_rows, width), bf16),
            pltpu.VMEM((fields * width, samples), bf16),
            pltpu.VMEM((groups, bags), f32),
            pltpu.VMEM((bag_len, bags), f32),
            pltpu.VMEM((half, bags), bf16),
            pltpu.VMEM((2 * width, bags), bf16),
            pltpu.VMEM((groups, half, 2 * width), bf16),
            pltpu.VMEM((groups, half, 2 * width), bf16),
            pltpu.VMEM((depth, folds * width), f32),
            dma((groups,)),
            dma((groups,)),
            dma((parts, folds)),
            dma((parts, folds)),
        ],
        compiler_params=pltpu.CompilerParams(
            collective_id=1, has_side_effects=True, vmem_limit_bytes=room
        ),
        name="scatter",
    )(pos, spread, own, w, rows, dinputs, lists, table, accum.reshape(table_rows // lane, lane))
    weight_grad = weight_grad.transpose(2, 0, 1)
    return (new_table, new_accum.reshape(table_rows), weight_grad)


def solution(mesh):
    placed = (
        P(("owner", "dense"), None, None),
        P(("owner", "dense"), None, None),
        P(("owner", "dense"), None, None),
        P(("owner", "dense")),
        P("owner", None),
        P("owner"),
        P(None, "dense"),
        P("dense"),
        P("dense"),
    )
    return jax.shard_map(
        local,
        mesh=mesh,
        in_specs=placed,
        out_specs=(P("owner", None), P("owner"), P(("owner", "dense"), None, None)),
        check_vma=False,
    )
```

```python
import functools

import jax
import jax.numpy as jnp
from jax import lax
from jax.experimental import pallas as pl
from jax.experimental.pallas import tpu as pltpu
from jax.sharding import PartitionSpec as P

step_size = 0.5
lane = 128
folds = 4
slab = 64
f32 = jnp.float32
bf16 = jnp.bfloat16
i32 = jnp.int32
MESH = pl.DeviceIdType.MESH
all_room = 64 * 1024 * 1024 - 128 * 1024


def vmem():
    return pl.BlockSpec(memory_space=pltpu.VMEM)


def partner(me, k, groups):
    peer = me
    bit = 1
    while bit < groups:
        flip = lax.rem(lax.div(k, bit), 2)
        peer = peer + bit * flip * (1 - 2 * lax.rem(lax.div(me, bit), 2))
        bit *= 2
    return peer


def in_waves(i, groups):
    half, quarter = groups // 2, groups // 4
    last = lax.div(i, quarter + half - 1)
    lower = jnp.where(i >= quarter, 1, 0) - last
    return i + (1 - lower - last) * half + lower * (1 - quarter) + last * 1


def in_turn(i, groups):
    odd = lax.rem(i, 2)
    return odd + lax.div(i, 2) + (1 - odd) * (groups // 2)


def name_rows(table_rows, uniq, own_ref, loc_ref, w_ref, row_ref, pos_ref, wo_ref, lows):
    bag_len, bags = own_ref.shape
    groups = pos_ref.shape[0]
    padded = row_ref.shape[1]
    highs = table_rows // lane
    counts = jnp.zeros((highs, lane), f32)
    low_at = lax.broadcasted_iota(i32, (lane, bags), 0)
    high_at = lax.broadcasted_iota(i32, (highs, bags), 0)
    for slot in range(bag_len):
        loc = loc_ref[slot : slot + 1, :]
        low = jnp.where(jnp.bitwise_and(loc, lane - 1) == low_at, 1.0, 0.0).astype(bf16)
        lows[slot] = low
        high = jnp.where(jnp.right_shift(loc, 7) == high_at, 1.0, 0.0).astype(bf16)
        counts += lax.dot_general(high, low, (((1,), (1,)), ((), ())), preferred_element_type=f32)
    present = jnp.where(counts > 0.0, 1.0, 0.0)
    upper = jnp.where(
        lax.broadcasted_iota(i32, (lane, lane), 0) <= lax.broadcasted_iota(i32, (lane, lane), 1),
        1.0,
        0.0,
    ).astype(bf16)
    below = jnp.where(
        lax.broadcasted_iota(i32, (highs, highs), 0) > lax.broadcasted_iota(i32, (highs, highs), 1),
        1.0,
        0.0,
    ).astype(bf16)
    inclusive = jnp.dot(present.astype(bf16), upper, preferred_element_type=f32)
    before = jnp.sum(
        jnp.dot(below, present.astype(bf16), preferred_element_type=f32), axis=1, keepdims=True
    )
    ranks = jnp.where(present > 0.0, inclusive + before - 1.0, -1.0)
    place = lax.broadcasted_iota(i32, (padded, lane), 0).astype(f32)
    lane_at = lax.broadcasted_iota(i32, (1, lane), 1).astype(f32)
    found = jnp.where(place < float(uniq), 0.0, -1.0)
    for h in range(highs):
        found += jnp.where(place == ranks[h : h + 1, :], lane_at + float(h * lane), 0.0)
    column = jnp.sum(found, axis=1, keepdims=True)
    column = jnp.where(place[:, :1] < float(uniq), column, -1.0)
    row_ref[...] = jnp.broadcast_to(column, (padded, lane)).T[0:1].astype(i32)
    whole = jnp.maximum(ranks, 0.0).astype(i32)
    both = jnp.concatenate(
        [jnp.right_shift(whole, 4), jnp.bitwise_and(whole, 15)], axis=0
    ).astype(f32).astype(bf16)
    owner_at = lax.broadcasted_iota(i32, (groups, bags), 0)
    named = jnp.full((groups, bags), -1, i32)
    weight = jnp.zeros((groups, bags), f32)
    for slot in range(bag_len):
        got = jnp.dot(both, lows[slot], preferred_element_type=f32)
        pick = jnp.right_shift(loc_ref[slot : slot + 1, :], 7) == high_at
        big = jnp.sum(jnp.where(pick, got[:highs], 0.0), axis=0, keepdims=True)
        small = jnp.sum(jnp.where(pick, got[highs:], 0.0), axis=0, keepdims=True)
        pos = (16.0 * big + small).astype(i32)
        hit = own_ref[slot : slot + 1, :] == owner_at
        named = jnp.where(hit, pos, named)
        weight = jnp.where(hit, w_ref[slot : slot + 1, :], weight)
    pos_ref[...] = named
    wo_ref[...] = weight


def greet(axis, count, peer_of):
    barrier = pltpu.get_barrier_semaphore()

    def hello(k, _):
        pl.semaphore_signal(
            barrier, inc=1, device_id={axis: peer_of(k)}, device_id_type=MESH
        )
        return 0

    lax.fori_loop(1, count, hello, 0)


def gather_body(
    groups, parts, fields, uniq, loads, early_loads, then, own_ref, loc_ref, w_ref, table_ref,
    win_ref, b_ref, o_ref, in_ref, rows_ref, lists_ref, pos_ref, wo_ref, wot_ref, bt_ref, ot_ref,
    row, lows, wide, found, acc, list_send, list_recv, send_sem, recv_sem,
    bo_send, bo_recv, y_send, y_recv, x_send, x_recv, s_send, s_recv, t_send, t_recv
):
    me = lax.axis_index("owner")
    lay = lax.axis_index("dense")
    samples = in_ref.shape[0]
    table_rows, width = table_ref.shape
    _, half, _ = rows_ref.shape
    padded = row.shape[1]
    depth = table_rows // folds
    greet("dense", parts, lambda k: lax.rem(lay + k, parts))
    greet("owner", groups, lambda k: partner(me, k, groups))
    for load in early_loads:
        load.start()
    pl.semaphore_wait(pltpu.get_barrier_semaphore(), groups + parts - 2)

    slabs = win_ref.shape[0] // slab
    passed = slabs // 5
    direct = slabs // 2 - passed
    core = lax.rem(me, 2)
    side = lax.rem(lax.div(me, 2), 2)

    def slab_of(its_side, its_core, i):
        j = 2 * i + its_core
        j = j + its_side * (slabs - 1 - 2 * j)
        return pl.ds(pl.multiple_of(j * slab, slab), slab)

    def y_copy(s, i):
        at = slab_of(side, core, i)
        return pltpu.make_async_remote_copy(
            src_ref=win_ref.at[at],
            dst_ref=wot_ref.at[s, at],
            send_sem=y_send.at[s - 1, i],
            recv_sem=y_recv.at[s - 1, i],
            device_id={"dense": lax.rem(lay + s, parts)},
            device_id_type=MESH,
        )

    def pass_on(s, at, i, k, send, recv):
        return pltpu.make_async_remote_copy(
            src_ref=wot_ref.at[s, at],
            dst_ref=wot_ref.at[s, at],
            send_sem=send.at[s - 1, i],
            recv_sem=recv.at[s - 1, i],
            device_id={"owner": partner(me, k, groups)},
            device_id_type=MESH,
        )

    def x_copy(s, i):
        return pass_on(s, slab_of(side, core, i), i, 2, x_send, x_recv)

    def s_copy(s, i):
        return pass_on(s, slab_of(side, core, i), i, 1, s_send, s_recv)

    def t_copy(s, i):
        return pass_on(s, slab_of(1 - side, core, i), i, 1, t_send, t_recv)

    def each_layer(act):
        for s in range(1, parts):
            act(s)

    def bo_copies(s):
        return [
            pltpu.make_async_remote_copy(
                src_ref=source,
                dst_ref=target.at[s],
                send_sem=bo_send.at[s - 1, i],
                recv_sem=bo_recv.at[s - 1, i],
                device_id={"dense": lax.rem(lay + s, parts)},
                device_id_type=MESH,
            )
            for i, (source, target) in enumerate(((b_ref, bt_ref), (o_ref, ot_ref)))
        ]

    def start_y(i, _):
        each_layer(lambda s: y_copy(s, i).start())
        return 0

    first = passed // 2
    second = 2 * first
    lax.fori_loop(0, first, start_y, 0)
    each_layer(lambda s: [copy.start() for copy in bo_copies(s)])

    def y_in(i, _):
        def act(s):
            y_copy(s, i).wait_recv()
            s_copy(s, i).start()

            @pl.when(i < passed)
            def _():
                x_copy(s, i).start()

        each_layer(act)
        return 0

    def x_in(i, _):
        def act(s):
            x_copy(s, i).wait_recv()
            t_copy(s, i).start()

        each_layer(act)
        return 0

    for load in loads:
        load.start()
    for load in early_loads[:3]:
        load.wait()
    own_ref[...] = jnp.bitwise_xor(own_ref[...], me)
    name_rows(table_rows, uniq, own_ref, loc_ref, w_ref, row, pos_ref, wo_ref, lows)
    lists_ref[0] = row[...]

    def list_copy(k):
        return pltpu.make_async_remote_copy(
            src_ref=row,
            dst_ref=lists_ref.at[k],
            send_sem=list_send.at[k],
            recv_sem=list_recv.at[k],
            device_id={"owner": partner(me, k, groups)},
            device_id_type=MESH,
        )

    def row_copy(k):
        return pltpu.make_async_remote_copy(
            src_ref=found.at[k],
            dst_ref=rows_ref.at[k],
            send_sem=send_sem.at[k],
            recv_sem=recv_sem.at[k],
            device_id={"owner": partner(me, k, groups)},
            device_id_type=MESH,
        )

    def send_list(i, _):
        list_copy(in_waves(i, groups)).start()
        return 0

    lax.fori_loop(0, groups - 1, send_list, 0)
    early_loads[3].wait()
    for j in range(folds):
        wide[:, j * width : (j + 1) * width] = table_ref[j * depth : (j + 1) * depth, :].astype(bf16)
    lane_at = lax.broadcasted_iota(i32, (2 * half, lane), 1)

    def look(k):
        ids = jnp.broadcast_to(lists_ref[k], (lane, padded)).T[: 2 * half]
        within = ids
        for j in range(1, folds):
            within = jnp.where(ids >= j * depth, ids - j * depth, within)
        pick = jnp.concatenate(
            [
                jnp.where(within - c * lane == lane_at, 1.0, 0.0).astype(bf16)
                for c in range(depth // lane)
            ],
            axis=1,
        )
        every = jnp.dot(pick, wide[...], preferred_element_type=f32)
        one = every[:, :width]
        for j in range(1, folds):
            one = jnp.where(ids >= j * depth, every[:, j * width : (j + 1) * width], one)
        one = one.astype(bf16)
        return jnp.concatenate([one[:half], one[half:]], axis=1)

    def serve(i, _):
        k = in_waves(i, groups)
        list_copy(k).wait_recv()
        found[k] = look(k)
        row_copy(k).start()
        return 0

    near = groups // 2
    lax.fori_loop(0, near, serve, 0)
    lax.fori_loop(first, second, start_y, 0)
    lax.fori_loop(near, groups - 1 - near // 2, serve, 0)
    rows_ref[0] = look(0)
    place = lax.broadcasted_iota(i32, (half, samples), 0)

    def pool(k):
        table_t = rows_ref[k].T
        for f in range(fields):
            at = slice(f * samples, (f + 1) * samples)
            pos = pos_ref[pl.ds(k, 1), at]
            upper = pos >= half
            pos = jnp.where(upper, pos - half, pos)
            mix = jnp.where(pos == place, wo_ref[pl.ds(k, 1), at], 0.0).astype(bf16)
            both = jnp.dot(table_t, mix, preferred_element_type=f32)
            rows = slice(f * width, (f + 1) * width)
            acc[rows, :] += jnp.where(upper, both[width:], both[:width])

    lax.fori_loop(0, first, y_in, 0)
    lax.fori_loop(second, passed, start_y, 0)
    acc[...] = jnp.zeros_like(acc)

    def take_near(k, _):
        @pl.when(k > 0)
        def _():
            row_copy(k).wait_recv()

        pool(k)
        return 0

    lax.fori_loop(0, near // 2, take_near, 0)
    lax.fori_loop(groups - 1 - near // 2, groups - 1, serve, 0)
    lax.fori_loop(near // 2, near, take_near, 0)
    lax.fori_loop(first, second, y_in, 0)
    lax.fori_loop(passed, direct, start_y, 0)
    lax.fori_loop(second, passed, y_in, 0)

    def take_far(j, _):
        row_copy(near + j).wait_recv()
        pool(near + j)
        return 0

    lax.fori_loop(0, near // 2, take_far, 0)
    lax.fori_loop(0, first, x_in, 0)
    lax.fori_loop(near // 2, near, take_far, 0)
    total = jnp.sum(wo_ref[...], axis=0, keepdims=True)
    for f in range(fields):
        pooled = acc[f * width : (f + 1) * width, :] / total[:, f * samples : (f + 1) * samples]
        in_ref[:, f * width : (f + 1) * width] = pooled.T.astype(bf16)

    lax.fori_loop(first, passed, x_in, 0)
    lax.fori_loop(passed, direct, y_in, 0)
    then()

    def finish(k, _):
        list_copy(k).wait_send()
        row_copy(k).wait_send()
        return 0

    lax.fori_loop(1, groups, finish, 0)
    each_layer(lambda s: [copy.wait() for copy in bo_copies(s)])

    def y_out(i, _):
        def act(s):
            y_copy(s, i).wait_send()
            s_copy(s, i).wait()

        each_layer(act)
        return 0

    def x_out(i, _):
        def act(s):
            x_copy(s, i).wait_send()
            t_copy(s, i).wait()

        each_layer(act)
        return 0

    lax.fori_loop(0, direct, y_out, 0)
    lax.fori_loop(0, passed, x_out, 0)


def spread(lines, c, block):
    return jnp.concatenate([lines[r : r + 1] for r in range(c // lane, (c + block) // lane)], axis=1)


def forward(p, block, x_ref, w_all, b_all, o_all, pre):
    biases, outs = b_all[p].astype(f32), o_all[p].astype(f32)
    part = jnp.zeros((x_ref.shape[0], lane), f32)
    for c in range(0, w_all.shape[2], block):
        at = slice(c, c + block)
        v = jnp.dot(x_ref[...], w_all[p, :, at], preferred_element_type=f32)
        v += spread(biases, c, block)
        pre[p, :, at] = v
        term = v * (0.5 + 0.5 * jnp.tanh(0.5 * v)) * spread(outs, c, block)
        for t in range(block // lane):
            part += term[:, t * lane : (t + 1) * lane]
    return part


def backward(block, part, label_ref, w_all, o_all, pre, out_ref):
    samples = part.shape[0]
    logits = jnp.sum(part, axis=1, keepdims=True)
    label = label_ref[...].astype(f32)
    label = jnp.concatenate(
        [
            jnp.broadcast_to(label[r : r + 1], (lane, lane)).T[:, :1]
            for r in range(samples // lane)
        ],
        axis=0,
    )
    grad = jax.nn.sigmoid(logits) - label
    for p in range(w_all.shape[0]):
        outs = o_all[p].astype(f32)
        for c in range(0, w_all.shape[2], block):
            at = slice(c, c + block)
            v = pre[p, :, at]
            sigma = 0.5 + 0.5 * jnp.tanh(0.5 * v)
            slope = sigma * (1.0 + v * (1.0 - sigma))
            dhidden = (grad * spread(outs, c, block) * slope).astype(bf16)
            term = lax.dot_general(
                w_all[p, :, at], dhidden, (((1,), (1,)), ((), ())), preferred_element_type=f32
            )
            if p == 0 and c == 0:
                out_ref[...] = term
            else:
                out_ref[...] += term


def scatter_body(
    groups, parts, fields, pos_ref, wo_ref, own_ref, w_ref, rows_ref, dp_ref, lists_ref,
    table_ref, accum_ref, wg_ref, new_table_ref, new_accum_ref, sums_ref, dp, scaled, along, mixes, dps, found, got, acc,
    send_sem, recv_sem, dense_send, dense_recv
):
    me = lax.axis_index("owner")
    lay = lax.axis_index("dense")
    bag_len, bags = own_ref.shape
    samples = bags // fields
    width = dp_ref.shape[0] // fields
    _, half, _ = rows_ref.shape
    padded = lists_ref.shape[2]
    depth = sums_ref.shape[1] // folds
    total = jnp.sum(w_ref[...], axis=0, keepdims=True)
    scaled[...] = wo_ref[...] / total
    along[...] = jnp.zeros_like(along)
    dp[...] = dp_ref[...].astype(bf16)
    acc[...] = jnp.zeros_like(acc)

    def grad_copy(k):
        return pltpu.make_async_remote_copy(
            src_ref=found.at[k],
            dst_ref=got.at[k],
            send_sem=send_sem.at[k],
            recv_sem=recv_sem.at[k],
            device_id={"owner": partner(me, k, groups)},
            device_id_type=MESH,
        )

    def dense_copy(k, j):
        return pltpu.make_async_remote_copy(
            src_ref=sums_ref.at[lay, pl.ds(j * depth, depth)],
            dst_ref=sums_ref.at[lay, pl.ds(j * depth, depth)],
            send_sem=dense_send.at[k, j],
            recv_sem=dense_recv.at[k, j],
            device_id={"dense": lax.rem(lay + k, parts)},
            device_id_type=MESH,
        )

    place = lax.broadcasted_iota(i32, (half, samples), 0)

    def grads(k):
        for f in range(fields):
            at = slice(f * samples, (f + 1) * samples)
            pos = pos_ref[pl.ds(k, 1), at]
            upper = pos >= half
            pos = jnp.where(upper, pos - half, pos)
            hit = pos == place
            mixes[:, at] = jnp.where(hit, scaled[pl.ds(k, 1), at], 0.0).astype(bf16)
            field = dp[f * width : (f + 1) * width, :]
            high = field * jnp.where(upper, 1.0, 0.0).astype(bf16)
            both = jnp.concatenate([field - high, high], axis=0)
            dps[:, at] = both
            dots = jnp.dot(rows_ref[k], both, preferred_element_type=f32)
            mine = jnp.sum(jnp.where(hit, dots, 0.0), axis=0, keepdims=True)
            along[:, at] += jnp.where(own_ref[:, at] == k, mine, 0.0)
        sums = lax.dot_general(
            dps[...], mixes[...], (((1,), (1,)), ((), ())), preferred_element_type=f32
        )
        return sums.T.astype(bf16)

    def give(i, _):
        k = in_turn(i, groups)
        found[k] = grads(k)
        grad_copy(k).start()
        return 0

    lax.fori_loop(0, groups - 1, give, 0)
    got[0] = grads(0)
    centre = jnp.sum(w_ref[...] * along[...], axis=0, keepdims=True) / total
    for f in range(fields):
        at = slice(f * samples, (f + 1) * samples)
        wg_ref[f] = (along[:, at] - centre[:, at]) / total[:, at]
    deep = lax.broadcasted_iota(i32, (depth, 2 * half), 0)

    def collect(k):
        row = lists_ref[k]
        ids = jnp.broadcast_to(row, (lane, padded)).T[: 2 * half]
        row = row[:, : 2 * half]
        within = row
        for j in range(1, folds):
            within = jnp.where(row >= j * depth, row - j * depth, within)
        pick = jnp.where(within == deep, 1.0, 0.0).astype(bf16)
        here = got[k].astype(f32)
        here = jnp.concatenate([here[:, :width], here[:, width:]], axis=0)
        split = jnp.concatenate(
            [
                jnp.where((ids >= j * depth) & (ids < (j + 1) * depth), here, 0.0).astype(bf16)
                for j in range(folds)
            ],
            axis=1,
        )
        acc[...] += jnp.dot(pick, split, preferred_element_type=f32)

    collect(0)

    def take(k, _):
        grad_copy(k).wait_recv()
        collect(k)
        return 0

    lax.fori_loop(1, groups, take, 0)
    for j in range(folds):
        sums_ref[lay, j * depth : (j + 1) * depth, :] = acc[:, j * width : (j + 1) * width].astype(bf16)
        for k in range(1, parts):
            dense_copy(k, j).start()

    rows_of = depth // lane
    for j in range(folds):
        for k in range(1, parts):
            dense_copy(k, j).wait_recv()
        for c in range(j * rows_of, (j + 1) * rows_of):
            at = slice(c * lane, (c + 1) * lane)
            total_grad = sums_ref[0, at, :].astype(f32)
            for p in range(1, parts):
                total_grad += sums_ref[p, at, :].astype(f32)
            square = (total_grad * total_grad).T
            grown = accum_ref[c : c + 1, :] + jnp.sum(square, axis=0, keepdims=True) * (1.0 / width)
            new_accum_ref[c : c + 1, :] = grown
            scale = jnp.broadcast_to(step_size * lax.rsqrt(grown), (lane, lane)).T
            new_table_ref[at, :] = table_ref[at, :] - total_grad * scale

    def finish(k, _):
        grad_copy(k).wait_send()
        return 0

    lax.fori_loop(1, groups, finish, 0)
    for k in range(1, parts):
        for j in range(folds):
            dense_copy(k, j).wait_send()


def whole_body(
    groups, parts, fields, uniq, block,
    own_hbm, loc_hbm, w_hbm, table_hbm, win_hbm, b_hbm, o_hbm, label_hbm, accum_hbm,
    wg_ref, new_table_ref, new_accum_ref,
    own, loc, w, table, w_all, b_all, o_all, label, accum, in_sems,
    x, rows, lists, pos, wo, row, lows, wide, found, acc, pre, dpooled,
    list_send, list_recv, send_sem, recv_sem, bo_send, bo_recv, y_send, y_recv,
    x_send, x_recv, s_send, s_recv, t_send, t_recv,
    sums, dp, scaled, along, mixes, dps, given, got, dense_acc,
    give_send, give_recv, dense_send, dense_recv
):
    pairs = (
        (loc_hbm, loc), (own_hbm, own), (w_hbm, w), (table_hbm, table),
        (win_hbm, w_all.at[0]), (b_hbm, b_all.at[0]), (o_hbm, o_all.at[0]),
        (label_hbm, label), (accum_hbm, accum),
    )
    loads = [
        pltpu.make_async_copy(source, target, in_sems.at[i])
        for i, (source, target) in enumerate(pairs)
    ]
    parts_of = []

    def own_part():
        for load in loads[4:]:
            load.wait()
        parts_of.append(forward(0, block, x, w_all, b_all, o_all, pre))

    gather_body(
        groups, parts, fields, uniq, loads[4:], loads[:4], own_part, own, loc, w, table,
        win_hbm, b_hbm, o_hbm, x, rows, lists, pos, wo, w_all, b_all, o_all,
        row, lows, wide, found, acc, list_send, list_recv, send_sem, recv_sem,
        bo_send, bo_recv, y_send, y_recv, x_send, x_recv, s_send, s_recv, t_send, t_recv,
    )
    part = parts_of[0]
    for p in range(1, parts):
        part += forward(p, block, x, w_all, b_all, o_all, pre)
    backward(block, part, label, w_all, o_all, pre, dpooled)
    scatter_body(
        groups, parts, fields, pos, wo, own, w, rows, dpooled, lists, table, accum,
        wg_ref, new_table_ref, new_accum_ref, sums, dp, scaled, along, mixes, dps,
        given, got, dense_acc, give_send, give_recv, dense_send, dense_recv,
    )


def local(owners, local_rows, weights, labels, table, accum, w_in, b_in, w_out):
    samples, fields, bag_len = owners.shape
    table_rows, width = table.shape
    groups = lax.axis_size("owner")
    parts = lax.axis_size("dense")
    bags = samples * fields
    uniq = bags * bag_len // (2 * groups)
    half = -(-uniq // 32) * 16
    padded = -(-2 * half // lane) * lane
    depth = table_rows // folds

    def by_slot(x):
        return x.transpose(2, 1, 0).reshape(bag_len, bags)

    own, loc, w = by_slot(owners), by_slot(local_rows), by_slot(weights)
    lines = w_in.shape[1] // lane
    bias, out_w = b_in.reshape(lines, lane), w_out.reshape(lines, lane)
    dma = pltpu.SemaphoreType.DMA
    hbm = pl.BlockSpec(memory_space=pltpu.HBM)
    wide, hidden = w_in.shape
    block = min(1024, hidden)
    layers = parts - 1
    passed = wide // slab // 5
    direct = wide // slab // 2 - passed
    rows_of = (groups, half, 2 * width)
    scratch = [
        pltpu.VMEM((bag_len, bags), i32),
        pltpu.VMEM((bag_len, bags), i32),
        pltpu.VMEM((bag_len, bags), f32),
        pltpu.VMEM((table_rows, width), f32),
        pltpu.VMEM((parts, wide, hidden), bf16),
        pltpu.VMEM((parts, lines, lane), bf16),
        pltpu.VMEM((parts, lines, lane), bf16),
        pltpu.VMEM((samples // lane, lane), bf16),
        pltpu.VMEM((table_rows // lane, lane), f32),
        dma((9,)),
        pltpu.VMEM((samples, fields * width), bf16),
        pltpu.VMEM(rows_of, bf16),
        pltpu.VMEM((groups, 1, padded), i32),
        pltpu.VMEM((groups, bags), i32),
        pltpu.VMEM((groups, bags), f32),
        pltpu.VMEM((1, padded), i32),
        pltpu.VMEM((bag_len, lane, bags), bf16),
        pltpu.VMEM((depth, folds * width), bf16),
        pltpu.VMEM(rows_of, bf16),
        pltpu.VMEM((fields * width, samples), f32),
        pltpu.VMEM((parts, samples, hidden), f32),
        pltpu.VMEM((fields * width, samples), f32),
        *[dma((groups,))] * 4,
        *[dma((layers, 2))] * 2,
        *[dma((layers, direct))] * 2,
        *[dma((layers, passed))] * 2,
        *[dma((layers, direct))] * 2,
        *[dma((layers, passed))] * 2,
        pltpu.VMEM((parts, table_rows, width), bf16),
        pltpu.VMEM((fields * width, samples), bf16),
        pltpu.VMEM((groups, bags), f32),
        pltpu.VMEM((bag_len, bags), f32),
        pltpu.VMEM((half, bags), bf16),
        pltpu.VMEM((2 * width, bags), bf16),
        pltpu.VMEM(rows_of, bf16),
        pltpu.VMEM(rows_of, bf16),
        pltpu.VMEM((depth, folds * width), f32),
        *[dma((groups,))] * 2,
        *[dma((parts, folds))] * 2,
    ]
    weight_grad, new_table, new_accum = pl.pallas_call(
        functools.partial(whole_body, groups, parts, fields, uniq, block),
        out_shape=(
            jax.ShapeDtypeStruct((fields, bag_len, samples), f32),
            jax.ShapeDtypeStruct((table_rows, width), f32),
            jax.ShapeDtypeStruct((table_rows // lane, lane), f32),
        ),
        in_specs=[hbm] * 9,
        out_specs=(vmem(),) * 3,
        scratch_shapes=scratch,
        compiler_params=pltpu.CompilerParams(
            collective_id=0, has_side_effects=True, vmem_limit_bytes=all_room
        ),
        name="whole",
    )(
        own, loc, w, table, w_in, bias, out_w,
        labels.reshape(-1, lane), accum.reshape(table_rows // lane, lane),
    )
    weight_grad = weight_grad.transpose(2, 0, 1)
    return (new_table, new_accum.reshape(table_rows), weight_grad)


def solution(mesh):
    placed = (
        P(("owner", "dense"), None, None),
        P(("owner", "dense"), None, None),
        P(("owner", "dense"), None, None),
        P(("owner", "dense")),
        P("owner", None),
        P("owner"),
        P(None, "dense"),
        P("dense"),
        P("dense"),
    )
    return jax.shard_map(
        local,
        mesh=mesh,
        in_specs=placed,
        out_specs=(P("owner", None), P("owner"), P(("owner", "dense"), None, None)),
        check_vma=False,
    )
```

```python
import functools

import jax
import jax.numpy as jnp
from jax import lax
from jax.experimental import pallas as pl
from jax.experimental.pallas import tpu as pltpu
from jax.sharding import PartitionSpec as P

step_size = 0.5
lane = 128
folds = 4
chunks = 4
slab = 64
f32 = jnp.float32
bf16 = jnp.bfloat16
i32 = jnp.int32
MESH = pl.DeviceIdType.MESH
all_room = 64 * 1024 * 1024 - 128 * 1024


def vmem():
    return pl.BlockSpec(memory_space=pltpu.VMEM)


def partner(me, k, groups):
    peer = me
    bit = 1
    while bit < groups:
        flip = lax.rem(lax.div(k, bit), 2)
        peer = peer + bit * flip * (1 - 2 * lax.rem(lax.div(me, bit), 2))
        bit *= 2
    return peer


def in_waves(i, groups):
    half, quarter = groups // 2, groups // 4
    last = lax.div(i, quarter + half - 1)
    lower = jnp.where(i >= quarter, 1, 0) - last
    return i + (1 - lower - last) * half + lower * (1 - quarter) + last * 1


def in_turn(i, groups):
    odd = lax.rem(i, 2)
    return odd + lax.div(i, 2) + (1 - odd) * (groups // 2)


def name_rows(table_rows, uniq, own_ref, loc_ref, w_ref, row_ref, pos_ref, wo_ref, lows):
    bag_len, bags = own_ref.shape
    groups = pos_ref.shape[0]
    padded = row_ref.shape[1]
    highs = table_rows // lane
    counts = jnp.zeros((highs, lane), f32)
    low_at = lax.broadcasted_iota(i32, (lane, bags), 0)
    high_at = lax.broadcasted_iota(i32, (highs, bags), 0)
    for slot in range(bag_len):
        loc = loc_ref[slot : slot + 1, :]
        low = jnp.where(jnp.bitwise_and(loc, lane - 1) == low_at, 1.0, 0.0).astype(bf16)
        lows[slot] = low
        high = jnp.where(jnp.right_shift(loc, 7) == high_at, 1.0, 0.0).astype(bf16)
        counts += lax.dot_general(high, low, (((1,), (1,)), ((), ())), preferred_element_type=f32)
    present = jnp.where(counts > 0.0, 1.0, 0.0)
    upper = jnp.where(
        lax.broadcasted_iota(i32, (lane, lane), 0) <= lax.broadcasted_iota(i32, (lane, lane), 1),
        1.0,
        0.0,
    ).astype(bf16)
    below = jnp.where(
        lax.broadcasted_iota(i32, (highs, highs), 0) > lax.broadcasted_iota(i32, (highs, highs), 1),
        1.0,
        0.0,
    ).astype(bf16)
    inclusive = jnp.dot(present.astype(bf16), upper, preferred_element_type=f32)
    before = jnp.sum(
        jnp.dot(below, present.astype(bf16), preferred_element_type=f32), axis=1, keepdims=True
    )
    ranks = jnp.where(present > 0.0, inclusive + before - 1.0, -1.0)
    place = lax.broadcasted_iota(i32, (padded, lane), 0).astype(f32)
    lane_at = lax.broadcasted_iota(i32, (1, lane), 1).astype(f32)
    found = jnp.where(place < float(uniq), 0.0, -1.0)
    for h in range(highs):
        found += jnp.where(place == ranks[h : h + 1, :], lane_at + float(h * lane), 0.0)
    column = jnp.sum(found, axis=1, keepdims=True)
    column = jnp.where(place[:, :1] < float(uniq), column, -1.0)
    row_ref[...] = jnp.broadcast_to(column, (padded, lane)).T[0:1].astype(i32)
    whole = jnp.maximum(ranks, 0.0).astype(i32)
    both = jnp.concatenate(
        [jnp.right_shift(whole, 4), jnp.bitwise_and(whole, 15)], axis=0
    ).astype(f32).astype(bf16)
    owner_at = lax.broadcasted_iota(i32, (groups, bags), 0)
    named = jnp.full((groups, bags), -1, i32)
    weight = jnp.zeros((groups, bags), f32)
    for slot in range(bag_len):
        got = jnp.dot(both, lows[slot], preferred_element_type=f32)
        pick = jnp.right_shift(loc_ref[slot : slot + 1, :], 7) == high_at
        big = jnp.sum(jnp.where(pick, got[:highs], 0.0), axis=0, keepdims=True)
        small = jnp.sum(jnp.where(pick, got[highs:], 0.0), axis=0, keepdims=True)
        pos = (16.0 * big + small).astype(i32)
        hit = own_ref[slot : slot + 1, :] == owner_at
        named = jnp.where(hit, pos, named)
        weight = jnp.where(hit, w_ref[slot : slot + 1, :], weight)
    pos_ref[...] = named
    wo_ref[...] = weight


def greet(groups, parts, me, lay):
    barrier = pltpu.get_barrier_semaphore()
    for s in range(parts):

        def hello(k, _):
            at = {"owner": partner(me, k, groups), "dense": lax.rem(lay + s, parts)}
            pl.semaphore_signal(barrier, inc=1, device_id=at, device_id_type=MESH)
            return 0

        lax.fori_loop(0 if s else 1, groups, hello, 0)


def gather_body(
    groups, parts, fields, uniq, loads, early_loads, then, own_ref, loc_ref, w_ref, table_ref,
    win_ref, b_ref, o_ref, in_ref, rows_ref, lists_ref, pos_ref, wo_ref, wot_ref, bt_ref, ot_ref,
    row, lows, wide, found, acc, list_send, list_recv, send_sem, recv_sem,
    bo_send, bo_recv, y_send, y_recv, x_send, x_recv, s_send, s_recv, t_send, t_recv
):
    me = lax.axis_index("owner")
    lay = lax.axis_index("dense")
    samples = in_ref.shape[0]
    table_rows, width = table_ref.shape
    _, half, _ = rows_ref.shape
    padded = row.shape[1]
    depth = table_rows // folds
    piece = width // parts
    greet(groups, parts, me, lay)
    for load in early_loads:
        load.start()
    pl.semaphore_wait(pltpu.get_barrier_semaphore(), groups * parts - 1)

    slabs = win_ref.shape[0] // slab
    passed = slabs // 5
    direct = slabs // 2 - passed
    core = lax.rem(me, 2)
    side = lax.rem(lax.div(me, 2), 2)

    def slab_of(its_side, its_core, i):
        j = 2 * i + its_core
        j = j + its_side * (slabs - 1 - 2 * j)
        return pl.ds(pl.multiple_of(j * slab, slab), slab)

    def y_copy(s, i):
        at = slab_of(side, core, i)
        return pltpu.make_async_remote_copy(
            src_ref=win_ref.at[at],
            dst_ref=wot_ref.at[s, at],
            send_sem=y_send.at[s - 1, i],
            recv_sem=y_recv.at[s - 1, i],
            device_id={"dense": lax.rem(lay + s, parts)},
            device_id_type=MESH,
        )

    def pass_on(s, at, i, k, send, recv):
        return pltpu.make_async_remote_copy(
            src_ref=wot_ref.at[s, at],
            dst_ref=wot_ref.at[s, at],
            send_sem=send.at[s - 1, i],
            recv_sem=recv.at[s - 1, i],
            device_id={"owner": partner(me, k, groups)},
            device_id_type=MESH,
        )

    def x_copy(s, i):
        return pass_on(s, slab_of(side, core, i), i, 2, x_send, x_recv)

    def s_copy(s, i):
        return pass_on(s, slab_of(side, core, i), i, 1, s_send, s_recv)

    def t_copy(s, i):
        return pass_on(s, slab_of(1 - side, core, i), i, 1, t_send, t_recv)

    def each_layer(act):
        for s in range(1, parts):
            act(s)

    def bo_copies(s):
        return [
            pltpu.make_async_remote_copy(
                src_ref=source,
                dst_ref=target.at[s],
                send_sem=bo_send.at[s - 1, i],
                recv_sem=bo_recv.at[s - 1, i],
                device_id={"dense": lax.rem(lay + s, parts)},
                device_id_type=MESH,
            )
            for i, (source, target) in enumerate(((b_ref, bt_ref), (o_ref, ot_ref)))
        ]

    def start_y(i, _):
        each_layer(lambda s: y_copy(s, i).start())
        return 0

    first = passed // 2
    second = 2 * first
    lax.fori_loop(0, first, start_y, 0)
    each_layer(lambda s: [copy.start() for copy in bo_copies(s)])

    def y_in(i, _):
        def act(s):
            y_copy(s, i).wait_recv()
            s_copy(s, i).start()

            @pl.when(i < passed)
            def _():
                x_copy(s, i).start()

        each_layer(act)
        return 0

    def x_in(i, _):
        def act(s):
            x_copy(s, i).wait_recv()
            t_copy(s, i).start()

        each_layer(act)
        return 0

    for load in loads:
        load.start()
    for load in early_loads[:3]:
        load.wait()
    own_ref[...] = jnp.bitwise_xor(own_ref[...], me)
    name_rows(table_rows, uniq, own_ref, loc_ref, w_ref, row, pos_ref, wo_ref, lows)
    lists_ref[lay, 0] = row[...]

    def list_copy(k, s, sender):
        return pltpu.make_async_remote_copy(
            src_ref=row,
            dst_ref=lists_ref.at[sender, k],
            send_sem=list_send.at[s, k],
            recv_sem=list_recv.at[sender, k],
            device_id={"owner": partner(me, k, groups), "dense": lax.rem(lay + s, parts)},
            device_id_type=MESH,
        )

    def row_copy(k):
        return pltpu.make_async_remote_copy(
            src_ref=found.at[k],
            dst_ref=rows_ref.at[k],
            send_sem=send_sem.at[k],
            recv_sem=recv_sem.at[k],
            device_id={"owner": partner(me, k, groups)},
            device_id_type=MESH,
        )

    def send_list(i, _):
        list_copy(in_waves(i, groups), 0, lay).start()
        return 0

    lax.fori_loop(0, groups - 1, send_list, 0)
    early_loads[3].wait()
    for j in range(folds):
        wide[:, j * width : (j + 1) * width] = table_ref[j * depth : (j + 1) * depth, :].astype(bf16)
    lane_at = lax.broadcasted_iota(i32, (2 * half, lane), 1)

    def look(k):
        ids = jnp.broadcast_to(lists_ref[lay, k], (lane, padded)).T[: 2 * half]
        within = ids
        for j in range(1, folds):
            within = jnp.where(ids >= j * depth, ids - j * depth, within)
        pick = jnp.concatenate(
            [
                jnp.where(within - c * lane == lane_at, 1.0, 0.0).astype(bf16)
                for c in range(depth // lane)
            ],
            axis=1,
        )
        every = jnp.dot(pick, wide[...], preferred_element_type=f32)
        one = every[:, :width]
        for j in range(1, folds):
            one = jnp.where(ids >= j * depth, every[:, j * width : (j + 1) * width], one)
        one = one.astype(bf16)
        return jnp.concatenate(
            [
                one[h * half : (h + 1) * half, d * piece : (d + 1) * piece]
                for d in range(parts)
                for h in range(2)
            ],
            axis=1,
        )

    def serve(i, _):
        k = in_waves(i, groups)
        list_copy(k, 0, lay).wait_recv()
        found[k] = look(k)
        row_copy(k).start()
        return 0

    near = groups // 2
    lax.fori_loop(0, near, serve, 0)
    lax.fori_loop(first, second, start_y, 0)
    lax.fori_loop(near, groups - 1 - near // 2, serve, 0)
    rows_ref[0] = look(0)

    def send_other_list(k, _):
        for s in range(1, parts):
            list_copy(k, s, lay).start()
        return 0

    lax.fori_loop(0, groups, send_other_list, 0)
    place = lax.broadcasted_iota(i32, (half, samples), 0)

    def pool(k):
        table_t = rows_ref[k].T
        for f in range(fields):
            at = slice(f * samples, (f + 1) * samples)
            pos = pos_ref[pl.ds(k, 1), at]
            upper = pos >= half
            pos = jnp.where(upper, pos - half, pos)
            mix = jnp.where(pos == place, wo_ref[pl.ds(k, 1), at], 0.0).astype(bf16)
            both = jnp.dot(table_t, mix, preferred_element_type=f32)
            rows = slice(f * width, (f + 1) * width)
            lower = [both[2 * d * piece : (2 * d + 1) * piece] for d in range(parts)]
            higher = [both[(2 * d + 1) * piece : (2 * d + 2) * piece] for d in range(parts)]
            acc[rows, :] += jnp.where(
                upper, jnp.concatenate(higher, axis=0), jnp.concatenate(lower, axis=0)
            )

    lax.fori_loop(0, first, y_in, 0)
    lax.fori_loop(second, passed, start_y, 0)
    acc[...] = jnp.zeros_like(acc)

    def take_near(k, _):
        @pl.when(k > 0)
        def _():
            row_copy(k).wait_recv()

        pool(k)
        return 0

    lax.fori_loop(0, near // 2, take_near, 0)
    lax.fori_loop(groups - 1 - near // 2, groups - 1, serve, 0)
    lax.fori_loop(near // 2, near, take_near, 0)
    lax.fori_loop(first, second, y_in, 0)
    lax.fori_loop(passed, direct, start_y, 0)
    lax.fori_loop(second, passed, y_in, 0)

    def take_far(j, _):
        row_copy(near + j).wait_recv()
        pool(near + j)
        return 0

    lax.fori_loop(0, near // 2, take_far, 0)
    lax.fori_loop(0, first, x_in, 0)
    lax.fori_loop(near // 2, near, take_far, 0)
    total = jnp.sum(wo_ref[...], axis=0, keepdims=True)
    for f in range(fields):
        pooled = acc[f * width : (f + 1) * width, :] / total[:, f * samples : (f + 1) * samples]
        in_ref[:, f * width : (f + 1) * width] = pooled.T.astype(bf16)

    lax.fori_loop(first, passed, x_in, 0)
    lax.fori_loop(passed, direct, y_in, 0)
    then()

    def finish(k, _):
        list_copy(k, 0, lay).wait_send()
        row_copy(k).wait_send()
        return 0

    lax.fori_loop(1, groups, finish, 0)

    def finish_other(k, _):
        for s in range(1, parts):
            sender = lax.rem(lay + s, parts)
            list_copy(k, s, lay).wait_send()
            list_copy(k, s, sender).wait_recv()
        return 0

    lax.fori_loop(0, groups, finish_other, 0)
    each_layer(lambda s: [copy.wait() for copy in bo_copies(s)])

    def y_out(i, _):
        def act(s):
            y_copy(s, i).wait_send()
            s_copy(s, i).wait()

        each_layer(act)
        return 0

    def x_out(i, _):
        def act(s):
            x_copy(s, i).wait_send()
            t_copy(s, i).wait()

        each_layer(act)
        return 0

    lax.fori_loop(0, direct, y_out, 0)
    lax.fori_loop(0, passed, x_out, 0)


def spread(lines, c, block):
    return jnp.concatenate([lines[r : r + 1] for r in range(c // lane, (c + block) // lane)], axis=1)


def forward(p, block, x_ref, w_all, b_all, o_all, pre):
    biases, outs = b_all[p].astype(f32), o_all[p].astype(f32)
    part = jnp.zeros((x_ref.shape[0], lane), f32)
    for c in range(0, w_all.shape[2], block):
        at = slice(c, c + block)
        v = jnp.dot(x_ref[...], w_all[p, :, at], preferred_element_type=f32)
        v += spread(biases, c, block)
        pre[p, :, at] = v
        term = v * (0.5 + 0.5 * jnp.tanh(0.5 * v)) * spread(outs, c, block)
        for t in range(block // lane):
            part += term[:, t * lane : (t + 1) * lane]
    return part


def backward(block, part, label_ref, w_all, o_all, pre, out_ref):
    samples = part.shape[0]
    logits = jnp.sum(part, axis=1, keepdims=True)
    label = label_ref[...].astype(f32)
    label = jnp.concatenate(
        [
            jnp.broadcast_to(label[r : r + 1], (lane, lane)).T[:, :1]
            for r in range(samples // lane)
        ],
        axis=0,
    )
    grad = jax.nn.sigmoid(logits) - label
    for p in range(w_all.shape[0]):
        outs = o_all[p].astype(f32)
        for c in range(0, w_all.shape[2], block):
            at = slice(c, c + block)
            v = pre[p, :, at]
            sigma = 0.5 + 0.5 * jnp.tanh(0.5 * v)
            slope = sigma * (1.0 + v * (1.0 - sigma))
            dhidden = (grad * spread(outs, c, block) * slope).astype(bf16)
            term = lax.dot_general(
                w_all[p, :, at], dhidden, (((1,), (1,)), ((), ())), preferred_element_type=f32
            )
            if p == 0 and c == 0:
                out_ref[...] = term
            else:
                out_ref[...] += term


def scatter_body(
    groups, parts, fields, pos_ref, wo_ref, own_ref, w_ref, rows_ref, dp_ref, lists_ref,
    wg_ref, sums_ref, dp, scaled, along, mixes, dps, found, got, acc,
    send_sem, recv_sem, dense_send, dense_recv
):
    me = lax.axis_index("owner")
    lay = lax.axis_index("dense")
    bag_len, bags = own_ref.shape
    samples = bags // fields
    width = dp_ref.shape[0] // fields
    _, half, _ = rows_ref.shape
    padded = lists_ref.shape[3]
    depth = sums_ref.shape[1]
    piece = width // parts
    per = lane // piece
    total = jnp.sum(w_ref[...], axis=0, keepdims=True)
    scaled[...] = wo_ref[...] / total
    along[...] = jnp.zeros_like(along)
    dp[...] = dp_ref[...].astype(bf16)
    acc[...] = jnp.zeros_like(acc)

    def grad_copy(k, s, sender):
        target = lax.rem(lay + s, parts)
        return pltpu.make_async_remote_copy(
            src_ref=found.at[target, k],
            dst_ref=got.at[sender, k],
            send_sem=send_sem.at[s, k],
            recv_sem=recv_sem.at[sender, k],
            device_id={"owner": partner(me, k, groups), "dense": target},
            device_id_type=MESH,
        )

    step = depth // chunks

    def dense_copy(k, j, sender):
        at = pl.ds(j * step, step)
        return pltpu.make_async_remote_copy(
            src_ref=sums_ref.at[lay, at],
            dst_ref=sums_ref.at[sender, at],
            send_sem=dense_send.at[k, j],
            recv_sem=dense_recv.at[k, j],
            device_id={"dense": lax.rem(lay + k, parts)},
            device_id_type=MESH,
        )

    place = lax.broadcasted_iota(i32, (half, samples), 0)

    def grads(k):
        for f in range(fields):
            at = slice(f * samples, (f + 1) * samples)
            pos = pos_ref[pl.ds(k, 1), at]
            upper = pos >= half
            pos = jnp.where(upper, pos - half, pos)
            hit = pos == place
            mixes[:, at] = jnp.where(hit, scaled[pl.ds(k, 1), at], 0.0).astype(bf16)
            field = dp[f * width : (f + 1) * width, :]
            high = field * jnp.where(upper, 1.0, 0.0).astype(bf16)
            low = field - high
            both = jnp.concatenate(
                [
                    which[d * piece : (d + 1) * piece]
                    for d in range(parts)
                    for which in (low, high)
                ],
                axis=0,
            )
            dps[:, at] = both
            dots = jnp.dot(rows_ref[k], both, preferred_element_type=f32)
            mine = jnp.sum(jnp.where(hit, dots, 0.0), axis=0, keepdims=True)
            along[:, at] += jnp.where(own_ref[:, at] == k, mine, 0.0)
        sums = lax.dot_general(
            dps[...], mixes[...], (((1,), (1,)), ((), ())), preferred_element_type=f32
        )
        sums = sums.T.astype(bf16)
        for d in range(parts):
            found[d, k] = sums[:, 2 * d * piece : 2 * (d + 1) * piece]

    def give(i, _):
        k = in_turn(i, groups)
        grads(k)
        for s in range(parts):
            grad_copy(k, s, lay).start()
        return 0

    lax.fori_loop(0, groups - 1, give, 0)
    grads(0)
    for s in range(1, parts):
        grad_copy(0, s, lay).start()
    got[lay, 0] = found[lay, 0]
    centre = jnp.sum(w_ref[...] * along[...], axis=0, keepdims=True) / total
    for f in range(fields):
        at = slice(f * samples, (f + 1) * samples)
        wg_ref[f] = (along[:, at] - centre[:, at]) / total[:, at]
    deep = lax.broadcasted_iota(i32, (depth, 2 * half), 0)

    first_row = lax.broadcasted_iota(i32, (1, lane), 1)
    first_row = sum([jnp.where(first_row >= d * piece, depth, 0) for d in range(1, per)])

    def collect(k):
        picks, splits = [], []
        for q in range(parts):
            row = lists_ref[q, k]
            ids = jnp.broadcast_to(row, (lane, padded)).T[: 2 * half]
            row = row[:, : 2 * half]
            within = row
            for j in range(1, folds):
                within = jnp.where(row >= j * depth, row - j * depth, within)
            picks.append(jnp.where(within == deep, 1.0, 0.0).astype(bf16))
            here = got[q, k].astype(f32)
            here = jnp.concatenate([here[:, :piece], here[:, piece:]], axis=0)
            here = jnp.concatenate([here] * per, axis=1)
            split = []
            for t in range(folds // per):
                base = first_row + t * per * depth
                inside = (ids >= base) & (ids < base + depth)
                split.append(jnp.where(inside, here, 0.0).astype(bf16))
            splits.append(jnp.concatenate(split, axis=1))
        acc[...] += jnp.dot(
            jnp.concatenate(picks, axis=1),
            jnp.concatenate(splits, axis=0),
            preferred_element_type=f32,
        )

    for s in range(1, parts):
        grad_copy(0, s, lax.rem(lay + s, parts)).wait_recv()
    collect(0)

    def take(k, _):
        for s in range(parts):
            grad_copy(k, s, lax.rem(lay + s, parts)).wait_recv()
        collect(k)
        return 0

    lax.fori_loop(1, groups, take, 0)
    for j in range(chunks):
        at = slice(j * step, (j + 1) * step)
        sums_ref[lay, at, :] = acc[at, :].astype(bf16)
        for k in range(1, parts):
            dense_copy(k, j, lay).start()
    for j in range(chunks):
        for k in range(1, parts):
            dense_copy(k, j, lax.rem(lay + parts - k, parts)).wait_recv()
    def finish(k, _):
        for s in range(parts):
            grad_copy(k, s, lay).wait_send()
        return 0

    for s in range(1, parts):
        grad_copy(0, s, lay).wait_send()
    lax.fori_loop(1, groups, finish, 0)
    for k in range(1, parts):
        for j in range(chunks):
            dense_copy(k, j, lay).wait_send()


def whole_body(
    groups, parts, fields, uniq, block,
    own_hbm, loc_hbm, w_hbm, table_hbm, win_hbm, b_hbm, o_hbm, label_hbm,
    wg_ref, sums,
    own, loc, w, table, w_all, b_all, o_all, label, in_sems,
    x, rows, lists, pos, wo, row, lows, wide, found, acc, pre, dpooled,
    list_send, list_recv, send_sem, recv_sem, bo_send, bo_recv, y_send, y_recv,
    x_send, x_recv, s_send, s_recv, t_send, t_recv,
    dp, scaled, along, mixes, dps, given, got, dense_acc,
    give_send, give_recv, dense_send, dense_recv
):
    pairs = (
        (loc_hbm, loc), (own_hbm, own), (w_hbm, w), (table_hbm, table),
        (win_hbm, w_all.at[0]), (b_hbm, b_all.at[0]), (o_hbm, o_all.at[0]),
        (label_hbm, label),
    )
    loads = [
        pltpu.make_async_copy(source, target, in_sems.at[i])
        for i, (source, target) in enumerate(pairs)
    ]
    parts_of = []

    def own_part():
        for load in loads[4:]:
            load.wait()
        parts_of.append(forward(0, block, x, w_all, b_all, o_all, pre))

    gather_body(
        groups, parts, fields, uniq, loads[4:], loads[:4], own_part, own, loc, w, table,
        win_hbm, b_hbm, o_hbm, x, rows, lists, pos, wo, w_all, b_all, o_all,
        row, lows, wide, found, acc, list_send, list_recv, send_sem, recv_sem,
        bo_send, bo_recv, y_send, y_recv, x_send, x_recv, s_send, s_recv, t_send, t_recv,
    )
    part = parts_of[0]
    for p in range(1, parts):
        part += forward(p, block, x, w_all, b_all, o_all, pre)
    backward(block, part, label, w_all, o_all, pre, dpooled)
    scatter_body(
        groups, parts, fields, pos, wo, own, w, rows, dpooled, lists,
        wg_ref, sums, dp, scaled, along, mixes, dps,
        given, got, dense_acc, give_send, give_recv, dense_send, dense_recv,
    )


def update_body(
    sums_hbm, table_hbm, accum_hbm, along_hbm, new_table_ref, new_accum_ref, wg_ref,
    sums, table, accum, sems
):
    pairs = ((sums_hbm, sums), (accum_hbm, accum), (table_hbm, table), (along_hbm, wg_ref))
    loads = [
        pltpu.make_async_copy(source, target, sems.at[i])
        for i, (source, target) in enumerate(pairs)
    ]
    for load in loads:
        load.start()
    for load in loads:
        load.wait()
    parts, depth, _ = sums.shape
    width = table.shape[1]
    piece = width // parts
    for c in range(depth // lane):
        got = [sums[d, c * lane : (c + 1) * lane, :].astype(f32) for d in range(parts)]
        for fold in range(folds):
            total = jnp.concatenate(
                [one[:, fold * piece : (fold + 1) * piece] for one in got], axis=1
            )
            line = fold * (depth // lane) + c
            at = slice(line * lane, (line + 1) * lane)
            square = jnp.sum((total * total).T, axis=0, keepdims=True)
            grown = accum[line : line + 1, :] + square * (1.0 / width)
            new_accum_ref[line : line + 1, :] = grown
            scale = jnp.broadcast_to(step_size * lax.rsqrt(grown), (lane, lane)).T
            new_table_ref[at, :] = table[at, :] - total * scale


def local(owners, local_rows, weights, labels, table, accum, w_in, b_in, w_out):
    samples, fields, bag_len = owners.shape
    table_rows, width = table.shape
    groups = lax.axis_size("owner")
    parts = lax.axis_size("dense")
    bags = samples * fields
    uniq = bags * bag_len // (2 * groups)
    half = -(-uniq // 32) * 16
    padded = -(-2 * half // lane) * lane
    depth = table_rows // folds

    def by_slot(x):
        return x.transpose(2, 1, 0).reshape(bag_len, bags)

    own, loc, w = by_slot(owners), by_slot(local_rows), by_slot(weights)
    lines = w_in.shape[1] // lane
    bias, out_w = b_in.reshape(lines, lane), w_out.reshape(lines, lane)
    dma = pltpu.SemaphoreType.DMA
    hbm = pl.BlockSpec(memory_space=pltpu.HBM)
    wide, hidden = w_in.shape
    block = min(1024, hidden)
    layers = parts - 1
    passed = wide // slab // 5
    direct = wide // slab // 2 - passed
    rows_of = (groups, half, 2 * width)
    piece = width // parts
    scratch = [
        pltpu.VMEM((bag_len, bags), i32),
        pltpu.VMEM((bag_len, bags), i32),
        pltpu.VMEM((bag_len, bags), f32),
        pltpu.VMEM((table_rows, width), f32),
        pltpu.VMEM((parts, wide, hidden), bf16),
        pltpu.VMEM((parts, lines, lane), bf16),
        pltpu.VMEM((parts, lines, lane), bf16),
        pltpu.VMEM((samples // lane, lane), bf16),
        dma((8,)),
        pltpu.VMEM((samples, fields * width), bf16),
        pltpu.VMEM(rows_of, bf16),
        pltpu.VMEM((parts, groups, 1, padded), i32),
        pltpu.VMEM((groups, bags), i32),
        pltpu.VMEM((groups, bags), f32),
        pltpu.VMEM((1, padded), i32),
        pltpu.VMEM((bag_len, lane, bags), bf16),
        pltpu.VMEM((depth, folds * width), bf16),
        pltpu.VMEM(rows_of, bf16),
        pltpu.VMEM((fields * width, samples), f32),
        pltpu.VMEM((parts, samples, hidden), f32),
        pltpu.VMEM((fields * width, samples), f32),
        *[dma((parts, groups))] * 2,
        *[dma((groups,))] * 2,
        *[dma((layers, 2))] * 2,
        *[dma((layers, direct))] * 2,
        *[dma((layers, passed))] * 2,
        *[dma((layers, direct))] * 2,
        *[dma((layers, passed))] * 2,
        pltpu.VMEM((fields * width, samples), bf16),
        pltpu.VMEM((groups, bags), f32),
        pltpu.VMEM((bag_len, bags), f32),
        pltpu.VMEM((half, bags), bf16),
        pltpu.VMEM((2 * width, bags), bf16),
        pltpu.VMEM((parts, groups, half, 2 * piece), bf16),
        pltpu.VMEM((parts, groups, half, 2 * piece), bf16),
        pltpu.VMEM((depth, folds * piece), f32),
        *[dma((parts, groups))] * 2,
        *[dma((parts, chunks))] * 2,
    ]
    weight_grad, sums = pl.pallas_call(
        functools.partial(whole_body, groups, parts, fields, uniq, block),
        out_shape=(
            jax.ShapeDtypeStruct((fields, bag_len, samples), f32),
            jax.ShapeDtypeStruct((parts, depth, folds * piece), bf16),
        ),
        in_specs=[hbm] * 8,
        out_specs=(vmem(),) * 2,
        scratch_shapes=scratch,
        compiler_params=pltpu.CompilerParams(
            collective_id=0, has_side_effects=True, vmem_limit_bytes=all_room
        ),
        name="whole",
    )(own, loc, w, table, w_in, bias, out_w, labels.reshape(-1, lane))
    new_table, new_accum, weight_grad = pl.pallas_call(
        update_body,
        out_shape=(
            jax.ShapeDtypeStruct((table_rows, width), f32),
            jax.ShapeDtypeStruct((table_rows // lane, lane), f32),
            jax.ShapeDtypeStruct((fields, bag_len, samples), f32),
        ),
        in_specs=[hbm] * 4,
        out_specs=(vmem(),) * 3,
        scratch_shapes=[
            pltpu.VMEM((parts, depth, folds * piece), bf16),
            pltpu.VMEM((table_rows, width), f32),
            pltpu.VMEM((table_rows // lane, lane), f32),
            dma((4,)),
        ],
        compiler_params=pltpu.CompilerParams(vmem_limit_bytes=all_room),
        name="update",
    )(sums, table, accum.reshape(table_rows // lane, lane), weight_grad)
    weight_grad = weight_grad.transpose(2, 0, 1)
    return (new_table, new_accum.reshape(table_rows), weight_grad)


def solution(mesh):
    placed = (
        P(("owner", "dense"), None, None),
        P(("owner", "dense"), None, None),
        P(("owner", "dense"), None, None),
        P(("owner", "dense")),
        P("owner", None),
        P("owner"),
        P(None, "dense"),
        P("dense"),
        P("dense"),
    )
    return jax.shard_map(
        local,
        mesh=mesh,
        in_specs=placed,
        out_specs=(P("owner", None), P("owner"), P(("owner", "dense"), None, None)),
        check_vma=False,
    )
```

```python
import functools

import jax
import jax.numpy as jnp
from jax import lax
from jax.experimental import pallas as pl
from jax.experimental.pallas import tpu as pltpu
from jax.sharding import PartitionSpec as P

step_size = 0.5
lane = 128
folds = 4
chunks = 4
slab = 64
f32 = jnp.float32
bf16 = jnp.bfloat16
i32 = jnp.int32
MESH = pl.DeviceIdType.MESH
all_room = 64 * 1024 * 1024 - 128 * 1024


def vmem():
    return pl.BlockSpec(memory_space=pltpu.VMEM)


def partner(me, k, groups):
    peer = me
    bit = 1
    while bit < groups:
        flip = lax.rem(lax.div(k, bit), 2)
        peer = peer + bit * flip * (1 - 2 * lax.rem(lax.div(me, bit), 2))
        bit *= 2
    return peer


def in_waves(i, groups):
    half, quarter = groups // 2, groups // 4
    last = lax.div(i, quarter + half - 1)
    lower = jnp.where(i >= quarter, 1, 0) - last
    return i + (1 - lower - last) * half + lower * (1 - quarter) + last * 1


def in_turn(i, groups):
    odd = lax.rem(i, 2)
    return odd + lax.div(i, 2) + (1 - odd) * (groups // 2)


def name_rows(table_rows, uniq, own_ref, loc_ref, w_ref, row_ref, pos_ref, wo_ref, lows):
    bag_len, bags = own_ref.shape
    groups = pos_ref.shape[0]
    padded = row_ref.shape[1]
    highs = table_rows // lane
    counts = jnp.zeros((highs, lane), f32)
    low_at = lax.broadcasted_iota(i32, (lane, bags), 0)
    high_at = lax.broadcasted_iota(i32, (highs, bags), 0)
    for slot in range(bag_len):
        loc = loc_ref[slot : slot + 1, :]
        low = jnp.where(jnp.bitwise_and(loc, lane - 1) == low_at, 1.0, 0.0).astype(bf16)
        lows[slot] = low
        high = jnp.where(jnp.right_shift(loc, 7) == high_at, 1.0, 0.0).astype(bf16)
        counts += lax.dot_general(high, low, (((1,), (1,)), ((), ())), preferred_element_type=f32)
    present = jnp.where(counts > 0.0, 1.0, 0.0)
    upper = jnp.where(
        lax.broadcasted_iota(i32, (lane, lane), 0) <= lax.broadcasted_iota(i32, (lane, lane), 1),
        1.0,
        0.0,
    ).astype(bf16)
    below = jnp.where(
        lax.broadcasted_iota(i32, (highs, highs), 0) > lax.broadcasted_iota(i32, (highs, highs), 1),
        1.0,
        0.0,
    ).astype(bf16)
    inclusive = jnp.dot(present.astype(bf16), upper, preferred_element_type=f32)
    before = jnp.sum(
        jnp.dot(below, present.astype(bf16), preferred_element_type=f32), axis=1, keepdims=True
    )
    ranks = jnp.where(present > 0.0, inclusive + before - 1.0, -1.0)
    place = lax.broadcasted_iota(i32, (padded, lane), 0).astype(f32)
    lane_at = lax.broadcasted_iota(i32, (1, lane), 1).astype(f32)
    found = jnp.where(place < float(uniq), 0.0, -1.0)
    for h in range(highs):
        found += jnp.where(place == ranks[h : h + 1, :], lane_at + float(h * lane), 0.0)
    column = jnp.sum(found, axis=1, keepdims=True)
    column = jnp.where(place[:, :1] < float(uniq), column, -1.0)
    row_ref[...] = jnp.broadcast_to(column, (padded, lane)).T[0:1].astype(i32)
    whole = jnp.maximum(ranks, 0.0).astype(i32)
    both = jnp.concatenate(
        [jnp.right_shift(whole, 4), jnp.bitwise_and(whole, 15)], axis=0
    ).astype(f32).astype(bf16)
    owner_at = lax.broadcasted_iota(i32, (groups, bags), 0)
    named = jnp.full((groups, bags), -1, i32)
    weight = jnp.zeros((groups, bags), f32)
    for slot in range(bag_len):
        got = jnp.dot(both, lows[slot], preferred_element_type=f32)
        pick = jnp.right_shift(loc_ref[slot : slot + 1, :], 7) == high_at
        big = jnp.sum(jnp.where(pick, got[:highs], 0.0), axis=0, keepdims=True)
        small = jnp.sum(jnp.where(pick, got[highs:], 0.0), axis=0, keepdims=True)
        pos = (16.0 * big + small).astype(i32)
        hit = own_ref[slot : slot + 1, :] == owner_at
        named = jnp.where(hit, pos, named)
        weight = jnp.where(hit, w_ref[slot : slot + 1, :], weight)
    pos_ref[...] = named
    wo_ref[...] = weight


def greet(groups, parts, me, lay):
    barrier = pltpu.get_barrier_semaphore()
    for s in range(parts):

        def hello(k, _):
            at = {"owner": partner(me, k, groups), "dense": lax.rem(lay + s, parts)}
            pl.semaphore_signal(barrier, inc=1, device_id=at, device_id_type=MESH)
            return 0

        lax.fori_loop(0 if s else 1, groups, hello, 0)


def gather_body(
    groups, parts, fields, uniq, loads, early_loads, then, own_ref, loc_ref, w_ref, table_ref,
    win_ref, b_ref, o_ref, in_ref, rows_ref, lists_ref, pos_ref, wo_ref, wot_ref, bt_ref, ot_ref,
    row, lows, wide, found, acc, list_send, list_recv, send_sem, recv_sem,
    bo_send, bo_recv, y_send, y_recv, x_send, x_recv, s_send, s_recv, t_send, t_recv
):
    me = lax.axis_index("owner")
    lay = lax.axis_index("dense")
    samples = in_ref.shape[0]
    table_rows, width = table_ref.shape
    _, half, _ = rows_ref.shape
    padded = row.shape[1]
    depth = table_rows // folds
    piece = width // parts
    greet(groups, parts, me, lay)
    for load in early_loads:
        load.start()
    pl.semaphore_wait(pltpu.get_barrier_semaphore(), groups * parts - 1)

    slabs = win_ref.shape[0] // slab
    passed = slabs // 4
    direct = slabs // 2 - passed
    core = lax.rem(me, 2)
    side = lax.rem(lax.div(me, 2), 2)

    def slab_of(its_side, its_core, i):
        j = 2 * i + its_core
        j = j + its_side * (slabs - 1 - 2 * j)
        return pl.ds(pl.multiple_of(j * slab, slab), slab)

    def y_copy(s, i):
        at = slab_of(side, core, i)
        return pltpu.make_async_remote_copy(
            src_ref=win_ref.at[at],
            dst_ref=wot_ref.at[s, at],
            send_sem=y_send.at[s - 1, i],
            recv_sem=y_recv.at[s - 1, i],
            device_id={"dense": lax.rem(lay + s, parts)},
            device_id_type=MESH,
        )

    def pass_on(s, at, i, k, send, recv):
        return pltpu.make_async_remote_copy(
            src_ref=wot_ref.at[s, at],
            dst_ref=wot_ref.at[s, at],
            send_sem=send.at[s - 1, i],
            recv_sem=recv.at[s - 1, i],
            device_id={"owner": partner(me, k, groups)},
            device_id_type=MESH,
        )

    def x_copy(s, i):
        return pass_on(s, slab_of(side, core, i), i, 2, x_send, x_recv)

    def s_copy(s, i):
        return pass_on(s, slab_of(side, core, i), i, 1, s_send, s_recv)

    def t_copy(s, i):
        return pass_on(s, slab_of(1 - side, core, i), i, 1, t_send, t_recv)

    def each_layer(act):
        for s in range(1, parts):
            act(s)

    def bo_copies(s):
        return [
            pltpu.make_async_remote_copy(
                src_ref=source,
                dst_ref=target.at[s],
                send_sem=bo_send.at[s - 1, i],
                recv_sem=bo_recv.at[s - 1, i],
                device_id={"dense": lax.rem(lay + s, parts)},
                device_id_type=MESH,
            )
            for i, (source, target) in enumerate(((b_ref, bt_ref), (o_ref, ot_ref)))
        ]

    def start_y(i, _):
        each_layer(lambda s: y_copy(s, i).start())
        return 0

    first = passed // 2
    second = 2 * first
    lax.fori_loop(0, first, start_y, 0)
    each_layer(lambda s: [copy.start() for copy in bo_copies(s)])

    def y_in(i, _):
        def act(s):
            y_copy(s, i).wait_recv()
            s_copy(s, i).start()

            @pl.when(i < passed)
            def _():
                x_copy(s, i).start()

        each_layer(act)
        return 0

    def x_in(i, _):
        def act(s):
            x_copy(s, i).wait_recv()
            t_copy(s, i).start()

        each_layer(act)
        return 0

    for load in loads:
        load.start()
    for load in early_loads[:3]:
        load.wait()
    own_ref[...] = jnp.bitwise_xor(own_ref[...], me)
    name_rows(table_rows, uniq, own_ref, loc_ref, w_ref, row, pos_ref, wo_ref, lows)
    lists_ref[lay, 0] = row[...]

    def list_copy(k, s, sender):
        return pltpu.make_async_remote_copy(
            src_ref=row,
            dst_ref=lists_ref.at[sender, k],
            send_sem=list_send.at[s, k],
            recv_sem=list_recv.at[sender, k],
            device_id={"owner": partner(me, k, groups), "dense": lax.rem(lay + s, parts)},
            device_id_type=MESH,
        )

    def row_copy(k):
        return pltpu.make_async_remote_copy(
            src_ref=found.at[k],
            dst_ref=rows_ref.at[k],
            send_sem=send_sem.at[k],
            recv_sem=recv_sem.at[k],
            device_id={"owner": partner(me, k, groups)},
            device_id_type=MESH,
        )

    def send_list(i, _):
        list_copy(in_waves(i, groups), 0, lay).start()
        return 0

    lax.fori_loop(0, groups - 1, send_list, 0)
    early_loads[3].wait()
    for j in range(folds):
        wide[:, j * width : (j + 1) * width] = table_ref[j * depth : (j + 1) * depth, :].astype(bf16)
    lane_at = lax.broadcasted_iota(i32, (2 * half, lane), 1)

    def look(k):
        ids = jnp.broadcast_to(lists_ref[lay, k], (lane, padded)).T[: 2 * half]
        within = ids
        for j in range(1, folds):
            within = jnp.where(ids >= j * depth, ids - j * depth, within)
        pick = jnp.concatenate(
            [
                jnp.where(within - c * lane == lane_at, 1.0, 0.0).astype(bf16)
                for c in range(depth // lane)
            ],
            axis=1,
        )
        every = jnp.dot(pick, wide[...], preferred_element_type=f32)
        one = every[:, :width]
        for j in range(1, folds):
            one = jnp.where(ids >= j * depth, every[:, j * width : (j + 1) * width], one)
        one = one.astype(bf16)
        return jnp.concatenate(
            [
                one[h * half : (h + 1) * half, d * piece : (d + 1) * piece]
                for d in range(parts)
                for h in range(2)
            ],
            axis=1,
        )

    def serve(i, _):
        k = in_waves(i, groups)
        list_copy(k, 0, lay).wait_recv()
        found[k] = look(k)
        row_copy(k).start()
        return 0

    near = groups // 2
    lax.fori_loop(0, near, serve, 0)
    lax.fori_loop(first, second, start_y, 0)
    lax.fori_loop(near, groups - 1 - near // 2, serve, 0)
    rows_ref[0] = look(0)

    def send_other_list(k, _):
        for s in range(1, parts):
            list_copy(k, s, lay).start()
        return 0

    lax.fori_loop(0, groups, send_other_list, 0)
    place = lax.broadcasted_iota(i32, (half, samples), 0)

    def pool(k):
        table_t = rows_ref[k].T
        for f in range(fields):
            at = slice(f * samples, (f + 1) * samples)
            pos = pos_ref[pl.ds(k, 1), at]
            upper = pos >= half
            pos = jnp.where(upper, pos - half, pos)
            mix = jnp.where(pos == place, wo_ref[pl.ds(k, 1), at], 0.0).astype(bf16)
            both = jnp.dot(table_t, mix, preferred_element_type=f32)
            rows = slice(f * width, (f + 1) * width)
            lower = [both[2 * d * piece : (2 * d + 1) * piece] for d in range(parts)]
            higher = [both[(2 * d + 1) * piece : (2 * d + 2) * piece] for d in range(parts)]
            acc[rows, :] += jnp.where(
                upper, jnp.concatenate(higher, axis=0), jnp.concatenate(lower, axis=0)
            )

    lax.fori_loop(0, first, y_in, 0)
    lax.fori_loop(second, passed, start_y, 0)
    acc[...] = jnp.zeros_like(acc)

    def take_near(k, _):
        @pl.when(k > 0)
        def _():
            row_copy(k).wait_recv()

        pool(k)
        return 0

    lax.fori_loop(0, near // 2, take_near, 0)
    lax.fori_loop(groups - 1 - near // 2, groups - 1, serve, 0)
    lax.fori_loop(near // 2, near, take_near, 0)
    lax.fori_loop(first, second, y_in, 0)
    lax.fori_loop(passed, direct, start_y, 0)
    lax.fori_loop(second, passed, y_in, 0)

    def take_far(j, _):
        row_copy(near + j).wait_recv()
        pool(near + j)
        return 0

    lax.fori_loop(0, near // 2, take_far, 0)
    lax.fori_loop(0, first, x_in, 0)
    lax.fori_loop(near // 2, near, take_far, 0)
    total = jnp.sum(wo_ref[...], axis=0, keepdims=True)
    for f in range(fields):
        pooled = acc[f * width : (f + 1) * width, :] / total[:, f * samples : (f + 1) * samples]
        in_ref[:, f * width : (f + 1) * width] = pooled.T.astype(bf16)

    lax.fori_loop(first, passed, x_in, 0)
    lax.fori_loop(passed, direct, y_in, 0)
    then()

    def finish(k, _):
        list_copy(k, 0, lay).wait_send()
        row_copy(k).wait_send()
        return 0

    lax.fori_loop(1, groups, finish, 0)

    def finish_other(k, _):
        for s in range(1, parts):
            sender = lax.rem(lay + s, parts)
            list_copy(k, s, lay).wait_send()
            list_copy(k, s, sender).wait_recv()
        return 0

    lax.fori_loop(0, groups, finish_other, 0)
    each_layer(lambda s: [copy.wait() for copy in bo_copies(s)])

    def y_out(i, _):
        def act(s):
            y_copy(s, i).wait_send()
            s_copy(s, i).wait()

        each_layer(act)
        return 0

    def x_out(i, _):
        def act(s):
            x_copy(s, i).wait_send()
            t_copy(s, i).wait()

        each_layer(act)
        return 0

    lax.fori_loop(0, direct, y_out, 0)
    lax.fori_loop(0, passed, x_out, 0)


def spread(lines, c, block):
    return jnp.concatenate([lines[r : r + 1] for r in range(c // lane, (c + block) // lane)], axis=1)


def forward(p, block, x_ref, w_all, b_all, o_all, pre):
    biases, outs = b_all[p].astype(f32), o_all[p].astype(f32)
    part = jnp.zeros((x_ref.shape[0], lane), f32)
    for c in range(0, w_all.shape[2], block):
        at = slice(c, c + block)
        v = jnp.dot(x_ref[...], w_all[p, :, at], preferred_element_type=f32)
        v += spread(biases, c, block)
        pre[p, :, at] = v
        term = v * (0.5 + 0.5 * jnp.tanh(0.5 * v)) * spread(outs, c, block)
        for t in range(block // lane):
            part += term[:, t * lane : (t + 1) * lane]
    return part


def backward(block, part, label_ref, w_all, o_all, pre, out_ref):
    samples = part.shape[0]
    logits = jnp.sum(part, axis=1, keepdims=True)
    label = label_ref[...].astype(f32)
    label = jnp.concatenate(
        [
            jnp.broadcast_to(label[r : r + 1], (lane, lane)).T[:, :1]
            for r in range(samples // lane)
        ],
        axis=0,
    )
    grad = jax.nn.sigmoid(logits) - label
    for p in range(w_all.shape[0]):
        outs = o_all[p].astype(f32)
        for c in range(0, w_all.shape[2], block):
            at = slice(c, c + block)
            v = pre[p, :, at]
            sigma = 0.5 + 0.5 * jnp.tanh(0.5 * v)
            slope = sigma * (1.0 + v * (1.0 - sigma))
            dhidden = (grad * spread(outs, c, block) * slope).astype(bf16)
            term = lax.dot_general(
                w_all[p, :, at], dhidden, (((1,), (1,)), ((), ())), preferred_element_type=f32
            )
            if p == 0 and c == 0:
                out_ref[...] = term
            else:
                out_ref[...] += term


def scatter_body(
    groups, parts, fields, pos_ref, wo_ref, own_ref, w_ref, rows_ref, dp_ref, lists_ref,
    wg_ref, sums_ref, dp, scaled, along, mixes, dps, found, got, acc,
    send_sem, recv_sem, dense_send, dense_recv
):
    me = lax.axis_index("owner")
    lay = lax.axis_index("dense")
    bag_len, bags = own_ref.shape
    samples = bags // fields
    width = dp_ref.shape[0] // fields
    _, half, _ = rows_ref.shape
    padded = lists_ref.shape[3]
    depth = sums_ref.shape[1]
    piece = width // parts
    per = lane // piece
    total = jnp.sum(w_ref[...], axis=0, keepdims=True)
    scaled[...] = wo_ref[...] / total
    along[...] = jnp.zeros_like(along)
    dp[...] = dp_ref[...].astype(bf16)
    acc[...] = jnp.zeros_like(acc)

    def grad_copy(k, s, sender):
        target = lax.rem(lay + s, parts)
        return pltpu.make_async_remote_copy(
            src_ref=found.at[target, k],
            dst_ref=got.at[sender, k],
            send_sem=send_sem.at[s, k],
            recv_sem=recv_sem.at[sender, k],
            device_id={"owner": partner(me, k, groups), "dense": target},
            device_id_type=MESH,
        )

    step = depth // chunks

    def dense_copy(k, j, sender):
        at = pl.ds(j * step, step)
        return pltpu.make_async_remote_copy(
            src_ref=sums_ref.at[lay, at],
            dst_ref=sums_ref.at[sender, at],
            send_sem=dense_send.at[k, j],
            recv_sem=dense_recv.at[k, j],
            device_id={"dense": lax.rem(lay + k, parts)},
            device_id_type=MESH,
        )

    place = lax.broadcasted_iota(i32, (half, samples), 0)

    def grads(k):
        for f in range(fields):
            at = slice(f * samples, (f + 1) * samples)
            pos = pos_ref[pl.ds(k, 1), at]
            upper = pos >= half
            pos = jnp.where(upper, pos - half, pos)
            hit = pos == place
            mixes[:, at] = jnp.where(hit, scaled[pl.ds(k, 1), at], 0.0).astype(bf16)
            field = dp[f * width : (f + 1) * width, :]
            high = field * jnp.where(upper, 1.0, 0.0).astype(bf16)
            low = field - high
            both = jnp.concatenate(
                [
                    which[d * piece : (d + 1) * piece]
                    for d in range(parts)
                    for which in (low, high)
                ],
                axis=0,
            )
            dps[:, at] = both
            dots = jnp.dot(rows_ref[k], both, preferred_element_type=f32)
            mine = jnp.sum(jnp.where(hit, dots, 0.0), axis=0, keepdims=True)
            along[:, at] += jnp.where(own_ref[:, at] == k, mine, 0.0)
        sums = lax.dot_general(
            dps[...], mixes[...], (((1,), (1,)), ((), ())), preferred_element_type=f32
        )
        sums = sums.T.astype(bf16)
        for d in range(parts):
            found[d, k] = sums[:, 2 * d * piece : 2 * (d + 1) * piece]

    def give(i, _):
        k = in_turn(i, groups)
        grads(k)
        for s in range(parts):
            grad_copy(k, s, lay).start()
        return 0

    lax.fori_loop(0, groups - 1, give, 0)
    grads(0)
    for s in range(1, parts):
        grad_copy(0, s, lay).start()
    got[lay, 0] = found[lay, 0]
    centre = jnp.sum(w_ref[...] * along[...], axis=0, keepdims=True) / total
    for f in range(fields):
        at = slice(f * samples, (f + 1) * samples)
        wg_ref[f] = (along[:, at] - centre[:, at]) / total[:, at]
    deep = lax.broadcasted_iota(i32, (depth, 2 * half), 0)

    first_row = lax.broadcasted_iota(i32, (1, lane), 1)
    first_row = sum([jnp.where(first_row >= d * piece, depth, 0) for d in range(1, per)])

    def collect(k):
        picks, splits = [], []
        for q in range(parts):
            row = lists_ref[q, k]
            ids = jnp.broadcast_to(row, (lane, padded)).T[: 2 * half]
            row = row[:, : 2 * half]
            within = row
            for j in range(1, folds):
                within = jnp.where(row >= j * depth, row - j * depth, within)
            picks.append(jnp.where(within == deep, 1.0, 0.0).astype(bf16))
            here = got[q, k].astype(f32)
            here = jnp.concatenate([here[:, :piece], here[:, piece:]], axis=0)
            here = jnp.concatenate([here] * per, axis=1)
            split = []
            for t in range(folds // per):
                base = first_row + t * per * depth
                inside = (ids >= base) & (ids < base + depth)
                split.append(jnp.where(inside, here, 0.0).astype(bf16))
            splits.append(jnp.concatenate(split, axis=1))
        acc[...] += jnp.dot(
            jnp.concatenate(picks, axis=1),
            jnp.concatenate(splits, axis=0),
            preferred_element_type=f32,
        )

    for s in range(1, parts):
        grad_copy(0, s, lax.rem(lay + s, parts)).wait_recv()
    collect(0)

    def take(k, _):
        for s in range(parts):
            grad_copy(k, s, lax.rem(lay + s, parts)).wait_recv()
        collect(k)
        return 0

    lax.fori_loop(1, groups, take, 0)
    for j in range(chunks):
        at = slice(j * step, (j + 1) * step)
        sums_ref[lay, at, :] = acc[at, :].astype(bf16)
        for k in range(1, parts):
            dense_copy(k, j, lay).start()
    for j in range(chunks):
        for k in range(1, parts):
            dense_copy(k, j, lax.rem(lay + parts - k, parts)).wait_recv()
    def finish(k, _):
        for s in range(parts):
            grad_copy(k, s, lay).wait_send()
        return 0

    for s in range(1, parts):
        grad_copy(0, s, lay).wait_send()
    lax.fori_loop(1, groups, finish, 0)
    for k in range(1, parts):
        for j in range(chunks):
            dense_copy(k, j, lay).wait_send()


def whole_body(
    groups, parts, fields, uniq, block,
    own_hbm, loc_hbm, w_hbm, table_hbm, win_hbm, b_hbm, o_hbm, label_hbm,
    wg_ref, sums,
    own, loc, w, table, w_all, b_all, o_all, label, in_sems,
    x, rows, lists, pos, wo, row, lows, wide, found, acc, pre, dpooled,
    list_send, list_recv, send_sem, recv_sem, bo_send, bo_recv, y_send, y_recv,
    x_send, x_recv, s_send, s_recv, t_send, t_recv,
    dp, scaled, along, mixes, dps, given, got, dense_acc,
    give_send, give_recv, dense_send, dense_recv
):
    pairs = (
        (loc_hbm, loc), (own_hbm, own), (w_hbm, w), (table_hbm, table),
        (win_hbm, w_all.at[0]), (b_hbm, b_all.at[0]), (o_hbm, o_all.at[0]),
        (label_hbm, label),
    )
    loads = [
        pltpu.make_async_copy(source, target, in_sems.at[i])
        for i, (source, target) in enumerate(pairs)
    ]
    parts_of = []

    def own_part():
        for load in loads[4:]:
            load.wait()
        parts_of.append(forward(0, block, x, w_all, b_all, o_all, pre))

    gather_body(
        groups, parts, fields, uniq, loads[4:], loads[:4], own_part, own, loc, w, table,
        win_hbm, b_hbm, o_hbm, x, rows, lists, pos, wo, w_all, b_all, o_all,
        row, lows, wide, found, acc, list_send, list_recv, send_sem, recv_sem,
        bo_send, bo_recv, y_send, y_recv, x_send, x_recv, s_send, s_recv, t_send, t_recv,
    )
    part = parts_of[0]
    for p in range(1, parts):
        part += forward(p, block, x, w_all, b_all, o_all, pre)
    backward(block, part, label, w_all, o_all, pre, dpooled)
    scatter_body(
        groups, parts, fields, pos, wo, own, w, rows, dpooled, lists,
        wg_ref, sums, dp, scaled, along, mixes, dps,
        given, got, dense_acc, give_send, give_recv, dense_send, dense_recv,
    )


def update_body(
    sums_hbm, table_hbm, accum_hbm, along_hbm, new_table_ref, new_accum_ref, wg_ref,
    sums, table, accum, sems
):
    pairs = ((sums_hbm, sums), (accum_hbm, accum), (table_hbm, table), (along_hbm, wg_ref))
    loads = [
        pltpu.make_async_copy(source, target, sems.at[i])
        for i, (source, target) in enumerate(pairs)
    ]
    for load in loads:
        load.start()
    for load in loads:
        load.wait()
    parts, depth, _ = sums.shape
    width = table.shape[1]
    piece = width // parts
    for c in range(depth // lane):
        got = [sums[d, c * lane : (c + 1) * lane, :].astype(f32) for d in range(parts)]
        for fold in range(folds):
            total = jnp.concatenate(
                [one[:, fold * piece : (fold + 1) * piece] for one in got], axis=1
            )
            line = fold * (depth // lane) + c
            at = slice(line * lane, (line + 1) * lane)
            square = jnp.sum((total * total).T, axis=0, keepdims=True)
            grown = accum[line : line + 1, :] + square * (1.0 / width)
            new_accum_ref[line : line + 1, :] = grown
            scale = jnp.broadcast_to(step_size * lax.rsqrt(grown), (lane, lane)).T
            new_table_ref[at, :] = table[at, :] - total * scale


def local(owners, local_rows, weights, labels, table, accum, w_in, b_in, w_out):
    samples, fields, bag_len = owners.shape
    table_rows, width = table.shape
    groups = lax.axis_size("owner")
    parts = lax.axis_size("dense")
    bags = samples * fields
    uniq = bags * bag_len // (2 * groups)
    half = -(-uniq // 32) * 16
    padded = -(-2 * half // lane) * lane
    depth = table_rows // folds

    def by_slot(x):
        return x.transpose(2, 1, 0).reshape(bag_len, bags)

    own, loc, w = by_slot(owners), by_slot(local_rows), by_slot(weights)
    lines = w_in.shape[1] // lane
    bias, out_w = b_in.reshape(lines, lane), w_out.reshape(lines, lane)
    dma = pltpu.SemaphoreType.DMA
    hbm = pl.BlockSpec(memory_space=pltpu.HBM)
    wide, hidden = w_in.shape
    block = min(1024, hidden)
    layers = parts - 1
    passed = wide // slab // 4
    direct = wide // slab // 2 - passed
    rows_of = (groups, half, 2 * width)
    piece = width // parts
    scratch = [
        pltpu.VMEM((bag_len, bags), i32),
        pltpu.VMEM((bag_len, bags), i32),
        pltpu.VMEM((bag_len, bags), f32),
        pltpu.VMEM((table_rows, width), f32),
        pltpu.VMEM((parts, wide, hidden), bf16),
        pltpu.VMEM((parts, lines, lane), bf16),
        pltpu.VMEM((parts, lines, lane), bf16),
        pltpu.VMEM((samples // lane, lane), bf16),
        dma((8,)),
        pltpu.VMEM((samples, fields * width), bf16),
        pltpu.VMEM(rows_of, bf16),
        pltpu.VMEM((parts, groups, 1, padded), i32),
        pltpu.VMEM((groups, bags), i32),
        pltpu.VMEM((groups, bags), f32),
        pltpu.VMEM((1, padded), i32),
        pltpu.VMEM((bag_len, lane, bags), bf16),
        pltpu.VMEM((depth, folds * width), bf16),
        pltpu.VMEM(rows_of, bf16),
        pltpu.VMEM((fields * width, samples), f32),
        pltpu.VMEM((parts, samples, hidden), f32),
        pltpu.VMEM((fields * width, samples), f32),
        *[dma((parts, groups))] * 2,
        *[dma((groups,))] * 2,
        *[dma((layers, 2))] * 2,
        *[dma((layers, direct))] * 2,
        *[dma((layers, passed))] * 2,
        *[dma((layers, direct))] * 2,
        *[dma((layers, passed))] * 2,
        pltpu.VMEM((fields * width, samples), bf16),
        pltpu.VMEM((groups, bags), f32),
        pltpu.VMEM((bag_len, bags), f32),
        pltpu.VMEM((half, bags), bf16),
        pltpu.VMEM((2 * width, bags), bf16),
        pltpu.VMEM((parts, groups, half, 2 * piece), bf16),
        pltpu.VMEM((parts, groups, half, 2 * piece), bf16),
        pltpu.VMEM((depth, folds * piece), f32),
        *[dma((parts, groups))] * 2,
        *[dma((parts, chunks))] * 2,
    ]
    weight_grad, sums = pl.pallas_call(
        functools.partial(whole_body, groups, parts, fields, uniq, block),
        out_shape=(
            jax.ShapeDtypeStruct((fields, bag_len, samples), f32),
            jax.ShapeDtypeStruct((parts, depth, folds * piece), bf16),
        ),
        in_specs=[hbm] * 8,
        out_specs=(vmem(),) * 2,
        scratch_shapes=scratch,
        compiler_params=pltpu.CompilerParams(
            collective_id=0, has_side_effects=True, vmem_limit_bytes=all_room
        ),
        name="whole",
    )(own, loc, w, table, w_in, bias, out_w, labels.reshape(-1, lane))
    new_table, new_accum, weight_grad = pl.pallas_call(
        update_body,
        out_shape=(
            jax.ShapeDtypeStruct((table_rows, width), f32),
            jax.ShapeDtypeStruct((table_rows // lane, lane), f32),
            jax.ShapeDtypeStruct((fields, bag_len, samples), f32),
        ),
        in_specs=[hbm] * 4,
        out_specs=(vmem(),) * 3,
        scratch_shapes=[
            pltpu.VMEM((parts, depth, folds * piece), bf16),
            pltpu.VMEM((table_rows, width), f32),
            pltpu.VMEM((table_rows // lane, lane), f32),
            dma((4,)),
        ],
        compiler_params=pltpu.CompilerParams(vmem_limit_bytes=all_room),
        name="update",
    )(sums, table, accum.reshape(table_rows // lane, lane), weight_grad)
    weight_grad = weight_grad.transpose(2, 0, 1)
    return (new_table, new_accum.reshape(table_rows), weight_grad)


def solution(mesh):
    placed = (
        P(("owner", "dense"), None, None),
        P(("owner", "dense"), None, None),
        P(("owner", "dense"), None, None),
        P(("owner", "dense")),
        P("owner", None),
        P("owner"),
        P(None, "dense"),
        P("dense"),
        P("dense"),
    )
    return jax.shard_map(
        local,
        mesh=mesh,
        in_specs=placed,
        out_specs=(P("owner", None), P("owner"), P(("owner", "dense"), None, None)),
        check_vma=False,
    )
```
